512 devices in a mesh: seq: 64 (over x, z, core), head: 8 (over y).
Axes of the slice: x: 4, y: 8, z: 8, core: 2. Of those that a mesh axis runs over, the one named last changes fastest.
Arguments:
- rotated_queries: bfloat16 [32768, 4096], P(('seq', 'head')), may hold values from -6 to 6
- rotated_keys: bfloat16 [32768, 2048], P(('seq', 'head')), may hold values from -6 to 6
- value_matrix: bfloat16 [32768, 2048], P(('seq', 'head')), may hold values from -6 to 6
- output_rows: bfloat16 [32768, 4096], P(('seq', 'head')), may hold values from -6 to 6
- output_gradient: bfloat16 [32768, 4096], P(('seq', 'head')), may hold values from -6 to 6
- softmax_log_total: float32 [32, 32768], P(None, ('seq', 'head')), may hold values from 4 to 7
- doc_ids: int32 [32768], replicated, may hold values from 0 to 32, never falling along the last dimension, each value on 1 to 2048 neighbouring positions
Outputs:
- query_grad: bfloat16 [32768, 4096], P('seq', 'head')
- key_grad: bfloat16 [32768, 2048], P('seq', 'head')
- value_grad: bfloat16 [32768, 2048], P('seq', 'head')
The draws below stay inside these ranges and needn't reach their ends.
Inputs may be any that keep to these rules, and one draw needn't show every extreme that they name: `doc_ids`: ids never fall from one token to the next; no document is longer than 2048 tokens.
All inputs are finite; a program needn't handle non-finite values.
Results may differ from the reference program's by a relative error of at most 0.0055.
Values may be sent and summed in bfloat16 or wider, within the bound.
No kernel may reach another device: no remote copies, remote signals or barrier semaphores. Data moves between devices by JAX's collectives and lax.ppermute only.
A program may use at most 64 MiB of HBM per device.

```python
import math
import jax
import jax.numpy as jnp
import numpy as np
from jax import lax

QUERY_HEADS = 32
KEY_VALUE_HEADS = 16
HEAD_SIZE = 128
LOOKBACK_SPAN = 1024
SEQUENCE_TOKENS = 512
SLAB_TOKENS = 32768


def level_of(rng, dims, shards, low, top_value):
    def one(axis_at, blocks):
        heights = jax.random.uniform(jax.random.fold_in(jax.random.fold_in(rng, 6), axis_at), (blocks,), jnp.float32, low / len(shards), top_value / len(shards))
        return jnp.repeat(jnp.exp(heights), dims[axis_at] // blocks).reshape((-1,) + (1,) * (len(dims) - axis_at - 1))

    factor_of = one(*shards[0])
    for cut in shards[1:]:
        factor_of = factor_of * one(*cut)
    return factor_of


def profile(count, total, bound, slope):
    loads = [(1 << 20) // math.isqrt(rank ** slope) + 1 for rank in range(2, count + 1)]
    spare, given = total - bound - (count - 1), [1] * (count - 1)
    while spare > 0:
        free = [i for i in range(count - 1) if given[i] < bound]
        whole, budget = sum([loads[i] for i in free]), spare
        for i in free:
            addition = min(bound - given[i], max(1, budget * loads[i] // whole), spare)
            given[i] = given[i] + addition
            spare = spare - addition
    return np.array([bound] + given)


def ragged_sizes(key, amount, total, limit, skew):
    if amount == 2:
        one = jax.random.randint(key, (), max(1, total - limit), min(limit, total - 1) + 1)
        return jnp.stack([one, total - one])
    lengths = jnp.asarray(profile(amount, total, limit, skew), jnp.int32)
    pairs = (amount - 1) // 2
    source_of, receiver = lengths[1:1 + 2 * pairs:2], lengths[2:2 + 2 * pairs:2]
    margin = jnp.minimum(source_of - 1, limit - receiver)
    passed = jax.random.randint(jax.random.fold_in(key, 1), (pairs,), 0, 1 << 20) % (margin + 1)
    lengths = lengths.at[1:1 + 2 * pairs:2].set(source_of - passed).at[2:2 + 2 * pairs:2].set(receiver + passed)
    return lengths[jax.random.permutation(jax.random.fold_in(key, 2), amount)]


def centred(rng, shape, deviation, limit, split=(), kind=jnp.bfloat16):
    result = jax.random.normal(rng, shape, jnp.float32) * deviation
    if len(split) > 0:
        result = level_of(rng, shape, split, -0.22, 0.18) * result
    return jnp.clip(result, min=-limit, max=limit).astype(kind)


def setup_inputs(seed: int = 0) -> dict:
    splits = jax.random.split(jax.random.key(seed), 8)
    rotated_queries = centred(splits[0], (SLAB_TOKENS, QUERY_HEADS * HEAD_SIZE), 1.0, 6.0, ((0, 512),))
    rotated_keys = centred(splits[1], (SLAB_TOKENS, KEY_VALUE_HEADS * HEAD_SIZE), 1.0, 6.0, ((0, 512),))
    value_matrix = centred(splits[2], (SLAB_TOKENS, KEY_VALUE_HEADS * HEAD_SIZE), 1.0, 6.0, ((0, 512),))
    output_rows = centred(splits[3], (SLAB_TOKENS, QUERY_HEADS * HEAD_SIZE), 1.0, 6.0, ((0, 512),))
    output_gradient = centred(splits[4], (SLAB_TOKENS, QUERY_HEADS * HEAD_SIZE), 1.0, 6.0, ((0, 512),))
    softmax_log_total = jnp.clip(4.0 + 3.0 * jax.random.uniform(splits[5], (QUERY_HEADS, SLAB_TOKENS), jnp.float32) ** level_of(splits[5], (QUERY_HEADS, SLAB_TOKENS), ((1, 512),), -0.2, 0.2), 4.0, 7.0)
    doc_ids = jnp.searchsorted(jnp.cumsum(ragged_sizes(splits[6], SLAB_TOKENS // (2 * SEQUENCE_TOKENS) + 1, SLAB_TOKENS, 4 * SEQUENCE_TOKENS, 2)), jnp.arange(SLAB_TOKENS), side="right").astype(jnp.int32)
    return dict(rotated_queries=rotated_queries, rotated_keys=rotated_keys, value_matrix=value_matrix, output_rows=output_rows, output_gradient=output_gradient, softmax_log_total=softmax_log_total, doc_ids=doc_ids)


score_scale = 168.0 ** -0.5


def reference(rotated_queries, rotated_keys, value_matrix, output_rows, output_gradient, softmax_log_total, doc_ids):
    number_of_tokens = rotated_queries.shape[0]
    window_extent = LOOKBACK_SPAN + SEQUENCE_TOKENS
    query_group_width = QUERY_HEADS // KEY_VALUE_HEADS
    delta_sum = jnp.einsum("thd,thd->ht", output_gradient.astype(jnp.float32).reshape(number_of_tokens, QUERY_HEADS, HEAD_SIZE),
                       output_rows.astype(jnp.float32).reshape(number_of_tokens, QUERY_HEADS, HEAD_SIZE))
    padded_keys = jnp.concatenate([jnp.zeros((LOOKBACK_SPAN, KEY_VALUE_HEADS * HEAD_SIZE), rotated_keys.dtype), rotated_keys], axis=0)
    padded_values = jnp.concatenate([jnp.zeros((LOOKBACK_SPAN, KEY_VALUE_HEADS * HEAD_SIZE), value_matrix.dtype), value_matrix], axis=0)
    doc_pad = jnp.concatenate([jnp.full((LOOKBACK_SPAN,), -1, jnp.int32), doc_ids.astype(jnp.int32)], axis=0)

    def one_block(carried, block_index):
        key_acc, value_acc = carried
        first_row_index = (block_index * SEQUENCE_TOKENS).astype(jnp.int32)
        query_piece = lax.dynamic_slice_in_dim(rotated_queries, first_row_index, SEQUENCE_TOKENS, 0).astype(jnp.float32).reshape(SEQUENCE_TOKENS, KEY_VALUE_HEADS, query_group_width, HEAD_SIZE)
        gradient_piece = lax.dynamic_slice_in_dim(output_gradient, first_row_index, SEQUENCE_TOKENS, 0).astype(jnp.float32).reshape(SEQUENCE_TOKENS, KEY_VALUE_HEADS, query_group_width, HEAD_SIZE)
        logsumexp_piece = lax.dynamic_slice_in_dim(softmax_log_total, first_row_index, SEQUENCE_TOKENS, 1).reshape(KEY_VALUE_HEADS, query_group_width, SEQUENCE_TOKENS)
        delta_piece = lax.dynamic_slice_in_dim(delta_sum, first_row_index, SEQUENCE_TOKENS, 1).reshape(KEY_VALUE_HEADS, query_group_width, SEQUENCE_TOKENS)
        key_piece = lax.dynamic_slice_in_dim(padded_keys, first_row_index, window_extent, 0).astype(jnp.float32).reshape(window_extent, KEY_VALUE_HEADS, HEAD_SIZE)
        value_piece = lax.dynamic_slice_in_dim(padded_values, first_row_index, window_extent, 0).astype(jnp.float32).reshape(window_extent, KEY_VALUE_HEADS, HEAD_SIZE)
        query_doc = lax.dynamic_slice_in_dim(doc_ids.astype(jnp.int32), first_row_index, SEQUENCE_TOKENS, 0)
        key_doc = lax.dynamic_slice_in_dim(doc_pad, first_row_index, window_extent, 0)
        query_pos = jnp.arange(SEQUENCE_TOKENS, dtype=jnp.int32) + LOOKBACK_SPAN
        key_pos = jnp.arange(window_extent, dtype=jnp.int32)
        gap = query_pos[:, None] - key_pos[None, :]
        allowed = (gap >= 0) & (gap < LOOKBACK_SPAN) & (query_doc[:, None] == key_doc[None, :])
        scores = jnp.einsum("rgad,cgd->garc", query_piece, key_piece) * score_scale
        prob_full = jnp.where(allowed[None, None], jnp.exp(scores - logsumexp_piece[..., None]), 0.0)
        probability_narrow = lax.optimization_barrier(prob_full.astype(jnp.bfloat16)).astype(jnp.float32)
        prob_grad = jnp.einsum("rgad,cgd->garc", gradient_piece, value_piece)
        score_gradient = (score_scale * prob_full * (prob_grad - delta_piece[..., None])).astype(jnp.bfloat16)
        score_gradient = lax.optimization_barrier(score_gradient).astype(jnp.float32)
        query_part = jnp.einsum("garc,cgd->rgad", score_gradient, key_piece).reshape(SEQUENCE_TOKENS, QUERY_HEADS * HEAD_SIZE)
        key_portion = jnp.einsum("plmw,mplo->wpo", score_gradient, query_piece).reshape(window_extent, KEY_VALUE_HEADS * HEAD_SIZE)
        value_portion = jnp.einsum("plmw,mplo->wpo", probability_narrow, gradient_piece).reshape(window_extent, KEY_VALUE_HEADS * HEAD_SIZE)
        key_acc = lax.dynamic_update_slice_in_dim(key_acc, lax.dynamic_slice_in_dim(key_acc, first_row_index, window_extent, 0) + key_portion, first_row_index, 0)
        value_acc = lax.dynamic_update_slice_in_dim(value_acc, lax.dynamic_slice_in_dim(value_acc, first_row_index, window_extent, 0) + value_portion, first_row_index, 0)
        return (key_acc, value_acc), query_part.astype(jnp.bfloat16)

    zero_accumulator = jnp.zeros((number_of_tokens + LOOKBACK_SPAN, KEY_VALUE_HEADS * HEAD_SIZE), jnp.float32)
    block_total = number_of_tokens // SEQUENCE_TOKENS
    (key_acc, value_acc), query_blocks = lax.scan(one_block, (zero_accumulator, zero_accumulator), jnp.arange(block_total, dtype=jnp.int32))
    query_grad = query_blocks.reshape(number_of_tokens, QUERY_HEADS * HEAD_SIZE)
    return query_grad, key_acc[LOOKBACK_SPAN:].astype(jnp.bfloat16), value_acc[LOOKBACK_SPAN:].astype(jnp.bfloat16)
```

```python
import math

import jax
import jax.numpy as jnp
from jax import lax
from jax.experimental import pallas as pl
from jax.experimental.pallas import tpu as pltpu
from jax.sharding import Mesh
from jax.sharding import PartitionSpec as P

HEAD_SIZE = 128
LOOKBACK_SPAN = 1024
CORES = 2
PIECE = 64
META_ROWS = 16
TILE = 256

score_scale = 168.0 ** (-0.5)
log2_e = math.log2(math.e)

f32 = jnp.float32
bf16 = jnp.bfloat16


def dot_t(left, right):
    return lax.dot_general(left, right, (((1,), (1,)), ((), ())), preferred_element_type=f32)


def dot_n(left, right):
    return lax.dot_general(left, right, (((1,), (0,)), ((), ())), preferred_element_type=f32)


def t_dot(left, right):
    return lax.dot_general(left, right, (((0,), (0,)), ((), ())), preferred_element_type=f32)


def pack_keys_kernel(key_ref, value_ref, out_ref):
    for at in range(CORES * out_ref.shape[1]):
        columns = slice(at * HEAD_SIZE, (at + 1) * HEAD_SIZE)
        out_ref[at % CORES, at // CORES, 0:PIECE, :] = key_ref[:, columns]
        out_ref[at % CORES, at // CORES, PIECE : 2 * PIECE, :] = value_ref[:, columns]


def pack_keys(keys, values, groups, steps=2):
    width = keys.shape[1] // steps
    return pl.pallas_call(
        pack_keys_kernel,
        grid=(steps,),
        in_specs=[pl.BlockSpec((PIECE, width), lambda i: (0, i))] * 2,
        out_specs=pl.BlockSpec((CORES, groups // steps, 2 * PIECE, HEAD_SIZE), lambda i: (0, i, 0, 0)),
        out_shape=jax.ShapeDtypeStruct((CORES, groups, 2 * PIECE, HEAD_SIZE), bf16),
        name="pack_keys",
    )(keys, values)


def three_parts(value):
    high = value.astype(bf16)
    rest = value - high.astype(f32)
    middle = rest.astype(bf16)
    return [high, middle, (rest - middle.astype(f32)).astype(bf16)]


def pack_queries_kernel(parity_ref, query_ref, grad_ref, row_ref, lse_ref, out_ref):
    groups = out_ref.shape[1]
    receivers = CORES * groups
    heads = 2 * receivers
    width = heads * HEAD_SIZE
    for at in range(receivers):
        for a in range(2):
            columns = slice((2 * at + a) * HEAD_SIZE, (2 * at + a + 1) * HEAD_SIZE)
            core, group = at % CORES, at // CORES
            out_ref[core, group, a * PIECE : (a + 1) * PIECE, :] = query_ref[:, columns]
            out_ref[core, group, (2 + a) * PIECE : (3 + a) * PIECE, :] = grad_ref[:, columns]
    product = grad_ref[...].astype(f32) * row_ref[...].astype(f32)
    product_high = product.astype(bf16)
    product_low = (product - product_high.astype(f32)).astype(bf16)
    which = lax.broadcasted_iota(jnp.int32, (heads, width), 1) // HEAD_SIZE
    member = jnp.where(which == lax.broadcasted_iota(jnp.int32, (heads, width), 0), 1.0, 0.0).astype(bf16)
    delta = dot_t(member, product_high) + dot_t(member, product_low)
    parts = three_parts(lse_ref[...]) + three_parts(delta)
    rows = jnp.concatenate([p.astype(f32) for p in parts], axis=0)
    rows = jnp.concatenate([rows, rows], axis=1)
    lane = lax.broadcasted_iota(jnp.int32, rows.shape, 1) // PIECE
    rows = jnp.where(lane == parity_ref[0], rows, 0.0).astype(bf16)
    total = receivers * META_ROWS
    row_at = lax.broadcasted_iota(jnp.int32, (total, 6 * heads), 0)
    column_at = lax.broadcasted_iota(jnp.int32, (total, 6 * heads), 1)
    receiver = (row_at // META_ROWS) % groups * CORES + row_at // (META_ROWS * groups)
    t = row_at % META_ROWS
    source = ((t // 6) * 3 + t % 3) * heads + 2 * receiver + (t // 3) % 2
    pick = jnp.where((t < 12) & (column_at == source), 1.0, 0.0).astype(bf16)
    meta = dot_n(pick, rows).astype(bf16)
    out_ref[:, :, 4 * PIECE : 4 * PIECE + META_ROWS, :] = meta.reshape(CORES, groups, META_ROWS, HEAD_SIZE)


def pack_queries(parity, queries, grads, rows, lse, groups, steps=4):
    width = queries.shape[1] // steps
    height = 4 * PIECE + META_ROWS
    return pl.pallas_call(
        pack_queries_kernel,
        grid=(steps,),
        in_specs=[pl.BlockSpec(memory_space=pltpu.SMEM)]
        + [pl.BlockSpec((PIECE, width), lambda i: (0, i))] * 3
        + [pl.BlockSpec((lse.shape[0] // steps, PIECE), lambda i: (i, 0))],
        out_specs=pl.BlockSpec((CORES, groups // steps, height, HEAD_SIZE), lambda i: (0, i, 0, 0)),
        out_shape=jax.ShapeDtypeStruct((CORES, groups, height, HEAD_SIZE), bf16),
        name="pack_queries",
    )(parity, queries, grads, rows, lse)


def sweep(causal, key_base, kv_ref, q_ref, lo_ref, meta_ref, dk_ref, dv_ref, dq_ref):
    pieces = TILE // PIECE
    tiles = LOOKBACK_SPAN // TILE

    meta = q_ref[:, 4 * PIECE : 4 * PIECE + META_ROWS, :].astype(f32)
    for p in range(LOOKBACK_SPAN // HEAD_SIZE):
        both = meta[2 * p] + meta[2 * p + 1]
        for r in range(4):
            one = both[3 * r : 3 * r + 1] + both[3 * r + 1 : 3 * r + 2] + both[3 * r + 2 : 3 * r + 3]
            meta_ref[p, r : r + 1, :] = one * log2_e if r < 2 else one

    dk_ref[...] = jnp.zeros_like(dk_ref)
    dv_ref[...] = jnp.zeros_like(dv_ref)

    def step(outer, inner):
        kt, qt = (inner, outer) if causal else (outer, inner)
        ks = kt * pieces
        qs = qt * pieces
        key = kv_ref[pl.ds(ks, pieces), 0:PIECE, :].reshape(TILE, HEAD_SIZE)
        value = kv_ref[pl.ds(ks, pieces), PIECE : 2 * PIECE, :].reshape(TILE, HEAD_SIZE)
        krows = pl.ds(pl.multiple_of(kt * TILE, TILE), TILE)
        qrows = pl.ds(pl.multiple_of(qt * TILE, TILE), TILE)
        key_at = lax.broadcasted_iota(jnp.int32, (TILE, TILE), 0)
        allowed = key_at >= lo_ref[qt] - (key_base + kt * TILE)
        if causal:
            query_at = lax.broadcasted_iota(jnp.int32, (TILE, TILE), 1)
            allowed = allowed & (key_at - query_at <= (qt - kt) * TILE)
        lanes = TILE // HEAD_SIZE
        dk = dk_ref[krows, :]
        dv = dv_ref[krows, :]
        for a in range(2):
            query = q_ref[pl.ds(qs, pieces), a * PIECE : (a + 1) * PIECE, :].reshape(TILE, HEAD_SIZE)
            grad = q_ref[pl.ds(qs, pieces), (2 + a) * PIECE : (3 + a) * PIECE, :].reshape(TILE, HEAD_SIZE)
            lse = jnp.concatenate([meta_ref[qt * lanes + i, a : a + 1, :] for i in range(lanes)], axis=1)
            delta = jnp.concatenate([meta_ref[qt * lanes + i, 2 + a : 3 + a, :] for i in range(lanes)], axis=1)
            scores = dot_t(key, query)
            prob = jnp.where(allowed, jnp.exp2(scores * (score_scale * log2_e) - lse), 0.0)
            prob_grad = dot_t(value, grad)
            score_grad = ((prob * score_scale) * (prob_grad - delta)).astype(bf16)
            dv = dv + dot_n(prob.astype(bf16), grad)
            dk = dk + dot_n(score_grad, query)
            dq_ref[a, qrows, :] = dq_ref[a, qrows, :] + t_dot(score_grad, key)
        dk_ref[krows, :] = dk
        dv_ref[krows, :] = dv

    for outer in range(tiles):
        lax.fori_loop(0, outer + 1, lambda inner, c, outer=outer: (step(outer, inner), c)[1], 0)


def cross_kernel(core_ref, kv_ref, q_ref, lo_ref, dq_ref, near_ref, far_ref, meta_ref, dk_ref, dv_ref):
    dq_ref[...] = jnp.zeros_like(dq_ref)
    sweep(False, 0, kv_ref, q_ref, lo_ref, meta_ref, dk_ref, dv_ref, dq_ref)
    half = LOOKBACK_SPAN // CORES
    near = pl.ds(pl.multiple_of(core_ref[0] * half, half), half)
    far = pl.ds(pl.multiple_of((1 - core_ref[0]) * half, half), half)
    near_ref[0] = dk_ref[near, :].astype(bf16)
    near_ref[1] = dv_ref[near, :].astype(bf16)
    far_ref[0] = dk_ref[far, :].astype(bf16)
    far_ref[1] = dv_ref[far, :].astype(bf16)


def own_kernel(kv_ref, q_ref, lo_ref, part_ref, out_ref, meta_ref, dk_ref, dv_ref, dq_ref):
    dq_ref[...] = part_ref[...]
    sweep(True, LOOKBACK_SPAN, kv_ref, q_ref, lo_ref, meta_ref, dk_ref, dv_ref, dq_ref)
    for core in range(CORES):
        block = slice(core * HALF, (core + 1) * HALF)
        out_ref[core, 0] = dq_ref[0, block, :].astype(bf16)
        out_ref[core, 1] = dq_ref[1, block, :].astype(bf16)
        out_ref[core, 2] = dk_ref[block, :].astype(bf16)
        out_ref[core, 3] = dv_ref[block, :].astype(bf16)


def vmem_spec():
    return pl.BlockSpec(memory_space=pltpu.VMEM)


def smem_spec():
    return pl.BlockSpec(memory_space=pltpu.SMEM)


SPAN_SCRATCH = [
    pltpu.VMEM((LOOKBACK_SPAN // HEAD_SIZE, 4, HEAD_SIZE), f32),
    pltpu.VMEM((LOOKBACK_SPAN, HEAD_SIZE), f32),
    pltpu.VMEM((LOOKBACK_SPAN, HEAD_SIZE), f32),
]
HALF = LOOKBACK_SPAN // CORES


def cost():
    pairs = LOOKBACK_SPAN * LOOKBACK_SPAN
    return pl.CostEstimate(flops=pairs * 5 * 2 * HEAD_SIZE, transcendentals=pairs, bytes_accessed=4 << 20)


def cross_terms(core, kv, q, lo):
    return pl.pallas_call(
        cross_kernel,
        in_specs=[smem_spec()] + [vmem_spec()] * 3,
        out_specs=[vmem_spec()] * 3,
        out_shape=[
            jax.ShapeDtypeStruct((2, LOOKBACK_SPAN, HEAD_SIZE), f32),
            jax.ShapeDtypeStruct((2, HALF, HEAD_SIZE), bf16),
            jax.ShapeDtypeStruct((2, HALF, HEAD_SIZE), bf16),
        ],
        scratch_shapes=SPAN_SCRATCH,
        compiler_params=pltpu.CompilerParams(vmem_limit_bytes=40 << 20),
        cost_estimate=cost(),
        name="cross_terms",
    )(core, kv, q, lo)


def own_terms(kv, q, lo, part):
    return pl.pallas_call(
        own_kernel,
        in_specs=[vmem_spec()] * 4,
        out_specs=vmem_spec(),
        out_shape=jax.ShapeDtypeStruct((CORES, 4, HALF, HEAD_SIZE), bf16),
        scratch_shapes=SPAN_SCRATCH + [pltpu.VMEM((2, LOOKBACK_SPAN, HEAD_SIZE), f32)],
        compiler_params=pltpu.CompilerParams(vmem_limit_bytes=40 << 20),
        cost_estimate=cost(),
        name="own_terms",
    )(kv, q, lo, part)


def join_kernel(core_ref, own_ref, near_ref, far_ref, dq_ref, dk_ref, dv_ref):
    for core in range(CORES):
        for a in range(2):
            at = 2 * core + a
            dq_ref[:, at * HEAD_SIZE : (at + 1) * HEAD_SIZE] = own_ref[core, a]

    for core in range(CORES):

        @pl.when(core_ref[0] == core)
        def _():
            for i, out_ref in enumerate((dk_ref, dv_ref)):
                for k in range(CORES):
                    back_ref = near_ref if k == core else far_ref
                    total = own_ref[k, 2 + i].astype(f32) + back_ref[i].astype(f32)
                    out_ref[:, k * HEAD_SIZE : (k + 1) * HEAD_SIZE] = total.astype(bf16)


def join(core, own, back_near, back_far):
    return pl.pallas_call(
        join_kernel,
        in_specs=[smem_spec()] + [vmem_spec()] * 3,
        out_specs=[vmem_spec()] * 3,
        out_shape=[
            jax.ShapeDtypeStruct((HALF, 4 * HEAD_SIZE), bf16),
            jax.ShapeDtypeStruct((HALF, 2 * HEAD_SIZE), bf16),
            jax.ShapeDtypeStruct((HALF, 2 * HEAD_SIZE), bf16),
        ],
        compiler_params=pltpu.CompilerParams(vmem_limit_bytes=16 << 20),
        name="join",
    )(core, own, back_near, back_far)


def first_allowed(doc_ids, chip):
    padded = jnp.concatenate([jnp.full((LOOKBACK_SPAN,), -1, jnp.int32), doc_ids])
    window = lax.dynamic_slice_in_dim(padded, chip * LOOKBACK_SPAN, 2 * LOOKBACK_SPAN, 0)
    own = window[LOOKBACK_SPAN:]
    document_start = jnp.sum((window[:, None] < own[None, :]).astype(jnp.int32), axis=0)
    reach_start = jnp.arange(1, LOOKBACK_SPAN + 1, dtype=jnp.int32)
    return jnp.maximum(document_start, reach_start).reshape(LOOKBACK_SPAN // TILE, 1, TILE)


def exchange(value):
    value = value.reshape((-1,) + value.shape[2:])
    return lax.all_to_all(value, ("core", "head"), split_axis=0, concat_axis=0, tiled=True)


def on_device(queries, keys, values, rows, grads, lse, doc_ids):
    chips = lax.axis_size("chip")
    groups = lax.axis_size("head")
    chip = lax.axis_index("chip")
    core = lax.axis_index("core").astype(jnp.int32).reshape(1)
    parity = (lax.axis_index("head") % 2).astype(jnp.int32).reshape(1)
    lo = first_allowed(doc_ids, chip)
    kv = exchange(pack_keys(keys, values, groups))
    packed = pack_queries(parity, queries, grads, rows, lse, groups)
    kv, packed = lax.optimization_barrier((kv, packed))
    q = exchange(packed)
    kv_before = lax.ppermute(kv, "chip", [(c, c + 1) for c in range(chips - 1)])
    dq_part, near, far = cross_terms(core, kv_before, q, lo)
    back_near = lax.ppermute(near, "chip", [(c + 1, c) for c in range(chips - 1)])
    back_far = lax.ppermute(
        far,
        ("chip", "core"),
        [(CORES * (c + 1) + k, CORES * c + 1 - k) for c in range(chips - 1) for k in range(CORES)],
    )
    own = own_terms(kv, q, lo, dq_part)
    own = lax.all_to_all(own, "core", split_axis=0, concat_axis=0, tiled=True)
    return join(core, own, back_near, back_far)


def solution(mesh):
    seq, head = mesh.devices.shape
    fine = Mesh(mesh.devices.reshape(seq // CORES, CORES, head), ("chip", "core", "head"))
    tokens = ("chip", "core", "head")
    return jax.shard_map(
        on_device,
        mesh=fine,
        in_specs=(P(tokens), P(tokens), P(tokens), P(tokens), P(tokens), P(None, tokens), P()),
        out_specs=(P(("chip", "core"), "head"),) * 3,
        check_vma=False,
    )
```

```python
import math

import jax
import jax.numpy as jnp
from jax import lax
from jax.experimental import pallas as pl
from jax.experimental.pallas import tpu as pltpu
from jax.sharding import Mesh
from jax.sharding import PartitionSpec as P

HEAD_SIZE = 128
LOOKBACK_SPAN = 1024
CORES = 2
PIECE = 64
META_ROWS = 16
CHUNK = 128

score_scale = 168.0 ** (-0.5)
log2_e = math.log2(math.e)

f32 = jnp.float32
bf16 = jnp.bfloat16


def dot_t(left, right):
    return lax.dot_general(left, right, (((1,), (1,)), ((), ())), preferred_element_type=f32)


def dot_n(left, right):
    return lax.dot_general(left, right, (((1,), (0,)), ((), ())), preferred_element_type=f32)


def t_dot(left, right):
    return lax.dot_general(left, right, (((0,), (0,)), ((), ())), preferred_element_type=f32)


def pack_keys_kernel(key_ref, value_ref, out_ref):
    for at in range(CORES * out_ref.shape[1]):
        columns = slice(at * HEAD_SIZE, (at + 1) * HEAD_SIZE)
        out_ref[at % CORES, at // CORES, 0:PIECE, :] = key_ref[:, columns]
        out_ref[at % CORES, at // CORES, PIECE : 2 * PIECE, :] = value_ref[:, columns]


def pack_keys(keys, values, groups, steps=2):
    width = keys.shape[1] // steps
    return pl.pallas_call(
        pack_keys_kernel,
        grid=(steps,),
        in_specs=[pl.BlockSpec((PIECE, width), lambda i: (0, i))] * 2,
        out_specs=pl.BlockSpec((CORES, groups // steps, 2 * PIECE, HEAD_SIZE), lambda i: (0, i, 0, 0)),
        out_shape=jax.ShapeDtypeStruct((CORES, groups, 2 * PIECE, HEAD_SIZE), bf16),
        name="pack_keys",
    )(keys, values)


def three_parts(value):
    high = value.astype(bf16)
    rest = value - high.astype(f32)
    middle = rest.astype(bf16)
    return [high, middle, (rest - middle.astype(f32)).astype(bf16)]


def pack_queries_kernel(parity_ref, query_ref, grad_ref, row_ref, lse_ref, out_ref):
    groups = out_ref.shape[1]
    receivers = CORES * groups
    heads = 2 * receivers
    width = heads * HEAD_SIZE
    for at in range(receivers):
        for a in range(2):
            columns = slice((2 * at + a) * HEAD_SIZE, (2 * at + a + 1) * HEAD_SIZE)
            core, group = at % CORES, at // CORES
            out_ref[core, group, a * PIECE : (a + 1) * PIECE, :] = query_ref[:, columns]
            out_ref[core, group, (2 + a) * PIECE : (3 + a) * PIECE, :] = grad_ref[:, columns]
    product = grad_ref[...].astype(f32) * row_ref[...].astype(f32)
    product_high = product.astype(bf16)
    product_low = (product - product_high.astype(f32)).astype(bf16)
    which = lax.broadcasted_iota(jnp.int32, (heads, width), 1) // HEAD_SIZE
    member = jnp.where(which == lax.broadcasted_iota(jnp.int32, (heads, width), 0), 1.0, 0.0).astype(bf16)
    delta = dot_t(member, product_high) + dot_t(member, product_low)
    parts = three_parts(lse_ref[...]) + three_parts(delta)
    rows = jnp.concatenate([p.astype(f32) for p in parts], axis=0)
    rows = jnp.concatenate([rows, rows], axis=1)
    lane = lax.broadcasted_iota(jnp.int32, rows.shape, 1) // PIECE
    rows = jnp.where(lane == parity_ref[0], rows, 0.0).astype(bf16)
    total = receivers * META_ROWS
    row_at = lax.broadcasted_iota(jnp.int32, (total, 6 * heads), 0)
    column_at = lax.broadcasted_iota(jnp.int32, (total, 6 * heads), 1)
    receiver = (row_at // META_ROWS) % groups * CORES + row_at // (META_ROWS * groups)
    t = row_at % META_ROWS
    source = ((t // 6) * 3 + t % 3) * heads + 2 * receiver + (t // 3) % 2
    pick = jnp.where((t < 12) & (column_at == source), 1.0, 0.0).astype(bf16)
    meta = dot_n(pick, rows).astype(bf16)
    out_ref[:, :, 4 * PIECE : 4 * PIECE + META_ROWS, :] = meta.reshape(CORES, groups, META_ROWS, HEAD_SIZE)


def pack_queries(parity, queries, grads, rows, lse, groups, steps=4):
    width = queries.shape[1] // steps
    height = 4 * PIECE + META_ROWS
    return pl.pallas_call(
        pack_queries_kernel,
        grid=(steps,),
        in_specs=[pl.BlockSpec(memory_space=pltpu.SMEM)]
        + [pl.BlockSpec((PIECE, width), lambda i: (0, i))] * 3
        + [pl.BlockSpec((lse.shape[0] // steps, PIECE), lambda i: (i, 0))],
        out_specs=pl.BlockSpec((CORES, groups // steps, height, HEAD_SIZE), lambda i: (0, i, 0, 0)),
        out_shape=jax.ShapeDtypeStruct((CORES, groups, height, HEAD_SIZE), bf16),
        name="pack_queries",
    )(parity, queries, grads, rows, lse)


def sweep(causal, key_base, kv_ref, q_ref, lo_ref, dk_ref, dv_ref, dq_ref, part_ref):
    pieces = CHUNK // PIECE
    chunks = LOOKBACK_SPAN // CHUNK
    order = range(chunks - 1, -1, -1) if causal else range(chunks)
    for n, at in enumerate(order):
        first, last = (0, at + 1) if causal else (at, chunks)
        strip = slice(first * CHUNK, last * CHUNK)
        height = (last - first) * CHUNK
        sources = slice(first * pieces, last * pieces)
        key = kv_ref[sources, 0:PIECE, :].reshape(height, HEAD_SIZE)
        value = kv_ref[sources, PIECE : 2 * PIECE, :].reshape(height, HEAD_SIZE)
        sources = slice(at * pieces, (at + 1) * pieces)

        def both(row):
            return jnp.concatenate(
                [q_ref[sources, (row + a) * PIECE : (row + a + 1) * PIECE, :].reshape(CHUNK, HEAD_SIZE) for a in range(2)]
            )

        query = both(0)
        grad = both(2)
        meta = q_ref[sources, 4 * PIECE : 4 * PIECE + META_ROWS, :].astype(f32)
        meta = meta[0] + meta[1]
        rows = [meta[3 * r : 3 * r + 1] + meta[3 * r + 1 : 3 * r + 2] + meta[3 * r + 2 : 3 * r + 3] for r in range(4)]
        lse = jnp.concatenate(rows[0:2], axis=1) * log2_e
        delta = jnp.concatenate(rows[2:4], axis=1)
        lo = lo_ref[at] - (key_base + first * CHUNK)
        lo = jnp.concatenate([lo, lo], axis=1)
        key_at = lax.broadcasted_iota(jnp.int32, (height, 2 * CHUNK), 0)
        allowed = key_at >= lo
        if causal:
            query_at = lax.broadcasted_iota(jnp.int32, (1, 2 * CHUNK), 1) % CHUNK + at * CHUNK
            allowed = allowed & (key_at <= query_at)
        scores = dot_t(key, query)
        prob = jnp.where(allowed, jnp.exp2(scores * (score_scale * log2_e) - lse), 0.0)
        prob_grad = dot_t(value, grad)
        score_grad = ((prob * score_scale) * (prob_grad - delta)).astype(bf16)
        dv = dot_n(prob.astype(bf16), grad)
        dk = dot_n(score_grad, query)
        if n == 0:
            dv_ref[strip, :] = dv
            dk_ref[strip, :] = dk
        else:
            dv_ref[strip, :] += dv
            dk_ref[strip, :] += dk
        dq = t_dot(score_grad, key)
        for a in range(2):
            mine = dq[a * CHUNK : (a + 1) * CHUNK]
            if part_ref is not None:
                mine = mine + part_ref[a, at * CHUNK : (at + 1) * CHUNK, :]
            dq_ref[a, at * CHUNK : (at + 1) * CHUNK, :] = mine


def cross_kernel(core_ref, kv_ref, q_ref, lo_ref, dq_ref, near_ref, far_ref, dk_ref, dv_ref):
    sweep(False, 0, kv_ref, q_ref, lo_ref, dk_ref, dv_ref, dq_ref, None)
    half = LOOKBACK_SPAN // CORES
    near = pl.ds(pl.multiple_of(core_ref[0] * half, half), half)
    far = pl.ds(pl.multiple_of((1 - core_ref[0]) * half, half), half)
    near_ref[0] = dk_ref[near, :].astype(bf16)
    near_ref[1] = dv_ref[near, :].astype(bf16)
    far_ref[0] = dk_ref[far, :].astype(bf16)
    far_ref[1] = dv_ref[far, :].astype(bf16)


def own_kernel(kv_ref, q_ref, lo_ref, part_ref, out_ref, dk_ref, dv_ref, dq_ref):
    sweep(True, LOOKBACK_SPAN, kv_ref, q_ref, lo_ref, dk_ref, dv_ref, dq_ref, part_ref)
    for core in range(CORES):
        block = slice(core * HALF, (core + 1) * HALF)
        out_ref[core, 0] = dq_ref[0, block, :].astype(bf16)
        out_ref[core, 1] = dq_ref[1, block, :].astype(bf16)
        out_ref[core, 2] = dk_ref[block, :].astype(bf16)
        out_ref[core, 3] = dv_ref[block, :].astype(bf16)


def vmem_spec():
    return pl.BlockSpec(memory_space=pltpu.VMEM)


def smem_spec():
    return pl.BlockSpec(memory_space=pltpu.SMEM)


SPAN_SCRATCH = [
    pltpu.VMEM((LOOKBACK_SPAN, HEAD_SIZE), f32),
    pltpu.VMEM((LOOKBACK_SPAN, HEAD_SIZE), f32),
]
HALF = LOOKBACK_SPAN // CORES


def cost():
    pairs = LOOKBACK_SPAN * LOOKBACK_SPAN
    return pl.CostEstimate(flops=pairs * 5 * 2 * HEAD_SIZE, transcendentals=pairs, bytes_accessed=4 << 20)


def cross_terms(core, kv, q, lo):
    return pl.pallas_call(
        cross_kernel,
        in_specs=[smem_spec()] + [vmem_spec()] * 3,
        out_specs=[vmem_spec()] * 3,
        out_shape=[
            jax.ShapeDtypeStruct((2, LOOKBACK_SPAN, HEAD_SIZE), f32),
            jax.ShapeDtypeStruct((2, HALF, HEAD_SIZE), bf16),
            jax.ShapeDtypeStruct((2, HALF, HEAD_SIZE), bf16),
        ],
        scratch_shapes=SPAN_SCRATCH,
        compiler_params=pltpu.CompilerParams(vmem_limit_bytes=40 << 20),
        cost_estimate=cost(),
        name="cross_terms",
    )(core, kv, q, lo)


def own_terms(kv, q, lo, part):
    return pl.pallas_call(
        own_kernel,
        in_specs=[vmem_spec()] * 4,
        out_specs=vmem_spec(),
        out_shape=jax.ShapeDtypeStruct((CORES, 4, HALF, HEAD_SIZE), bf16),
        scratch_shapes=SPAN_SCRATCH + [pltpu.VMEM((2, LOOKBACK_SPAN, HEAD_SIZE), f32)],
        compiler_params=pltpu.CompilerParams(vmem_limit_bytes=40 << 20),
        cost_estimate=cost(),
        name="own_terms",
    )(kv, q, lo, part)


def join_kernel(core_ref, own_ref, near_ref, far_ref, dq_ref, dk_ref, dv_ref):
    for core in range(CORES):
        for a in range(2):
            at = 2 * core + a
            dq_ref[:, at * HEAD_SIZE : (at + 1) * HEAD_SIZE] = own_ref[core, a]

    for core in range(CORES):

        @pl.when(core_ref[0] == core)
        def _():
            for i, out_ref in enumerate((dk_ref, dv_ref)):
                for k in range(CORES):
                    back_ref = near_ref if k == core else far_ref
                    total = own_ref[k, 2 + i].astype(f32) + back_ref[i].astype(f32)
                    out_ref[:, k * HEAD_SIZE : (k + 1) * HEAD_SIZE] = total.astype(bf16)


def join(core, own, back_near, back_far):
    return pl.pallas_call(
        join_kernel,
        in_specs=[smem_spec()] + [vmem_spec()] * 3,
        out_specs=[vmem_spec()] * 3,
        out_shape=[
            jax.ShapeDtypeStruct((HALF, 4 * HEAD_SIZE), bf16),
            jax.ShapeDtypeStruct((HALF, 2 * HEAD_SIZE), bf16),
            jax.ShapeDtypeStruct((HALF, 2 * HEAD_SIZE), bf16),
        ],
        compiler_params=pltpu.CompilerParams(vmem_limit_bytes=16 << 20),
        name="join",
    )(core, own, back_near, back_far)


def first_allowed(doc_ids, chip):
    padded = jnp.concatenate([jnp.full((LOOKBACK_SPAN,), -1, jnp.int32), doc_ids])
    window = lax.dynamic_slice_in_dim(padded, chip * LOOKBACK_SPAN, 2 * LOOKBACK_SPAN, 0)
    own = window[LOOKBACK_SPAN:]
    document_start = jnp.sum((window[:, None] < own[None, :]).astype(jnp.int32), axis=0)
    reach_start = jnp.arange(1, LOOKBACK_SPAN + 1, dtype=jnp.int32)
    return jnp.maximum(document_start, reach_start).reshape(LOOKBACK_SPAN // CHUNK, 1, CHUNK)


def exchange(value):
    value = value.reshape((-1,) + value.shape[2:])
    return lax.all_to_all(value, ("core", "head"), split_axis=0, concat_axis=0, tiled=True)


def on_device(queries, keys, values, rows, grads, lse, doc_ids):
    chips = lax.axis_size("chip")
    groups = lax.axis_size("head")
    chip = lax.axis_index("chip")
    core = lax.axis_index("core").astype(jnp.int32).reshape(1)
    parity = (lax.axis_index("head") % 2).astype(jnp.int32).reshape(1)
    lo = first_allowed(doc_ids, chip)
    kv = exchange(pack_keys(keys, values, groups))
    packed = pack_queries(parity, queries, grads, rows, lse, groups)
    kv, packed = lax.optimization_barrier((kv, packed))
    q = exchange(packed)
    kv_before = lax.ppermute(kv, "chip", [(c, c + 1) for c in range(chips - 1)])
    dq_part, near, far = cross_terms(core, kv_before, q, lo)
    back_near = lax.ppermute(near, "chip", [(c + 1, c) for c in range(chips - 1)])
    back_far = lax.ppermute(
        far,
        ("chip", "core"),
        [(CORES * (c + 1) + k, CORES * c + 1 - k) for c in range(chips - 1) for k in range(CORES)],
    )
    own = own_terms(kv, q, lo, dq_part)
    own = lax.all_to_all(own, "core", split_axis=0, concat_axis=0, tiled=True)
    return join(core, own, back_near, back_far)


def solution(mesh):
    seq, head = mesh.devices.shape
    fine = Mesh(mesh.devices.reshape(seq // CORES, CORES, head), ("chip", "core", "head"))
    tokens = ("chip", "core", "head")
    return jax.shard_map(
        on_device,
        mesh=fine,
        in_specs=(P(tokens), P(tokens), P(tokens), P(tokens), P(tokens), P(None, tokens), P()),
        out_specs=(P(("chip", "core"), "head"),) * 3,
        check_vma=False,
    )
```

```python
import functools
import math

import jax
import jax.numpy as jnp
from jax import lax
from jax.experimental import pallas as pl
from jax.experimental.pallas import tpu as pltpu
from jax.sharding import Mesh
from jax.sharding import PartitionSpec as P

HEAD_SIZE = 128
LOOKBACK_SPAN = 1024
CORES = 2
PIECE = 64
META_ROWS = 16
CHUNK = 128

score_scale = 168.0 ** (-0.5)
log2_e = math.log2(math.e)

f32 = jnp.float32
bf16 = jnp.bfloat16


def dot_t(left, right):
    return lax.dot_general(left, right, (((1,), (1,)), ((), ())), preferred_element_type=f32)


def dot_n(left, right):
    return lax.dot_general(left, right, (((1,), (0,)), ((), ())), preferred_element_type=f32)


def t_dot(left, right):
    return lax.dot_general(left, right, (((0,), (0,)), ((), ())), preferred_element_type=f32)


def pack_keys_kernel(key_ref, value_ref, out_ref):
    for at in range(CORES * out_ref.shape[1]):
        columns = slice(at * HEAD_SIZE, (at + 1) * HEAD_SIZE)
        out_ref[at % CORES, at // CORES, 0:PIECE, :] = key_ref[:, columns]
        out_ref[at % CORES, at // CORES, PIECE : 2 * PIECE, :] = value_ref[:, columns]


def pack_keys(keys, values, groups, steps=2):
    width = keys.shape[1] // steps
    return pl.pallas_call(
        pack_keys_kernel,
        grid=(steps,),
        in_specs=[pl.BlockSpec((PIECE, width), lambda i: (0, i))] * 2,
        out_specs=pl.BlockSpec((CORES, groups // steps, 2 * PIECE, HEAD_SIZE), lambda i: (0, i, 0, 0)),
        out_shape=jax.ShapeDtypeStruct((CORES, groups, 2 * PIECE, HEAD_SIZE), bf16),
        name="pack_keys",
    )(keys, values)


def three_parts(value):
    high = value.astype(bf16)
    rest = value - high.astype(f32)
    middle = rest.astype(bf16)
    return [high, middle, (rest - middle.astype(f32)).astype(bf16)]


def pack_queries_kernel(parity_ref, query_ref, grad_ref, row_ref, lse_ref, out_ref):
    groups = out_ref.shape[1]
    receivers = CORES * groups
    heads = 2 * receivers
    width = heads * HEAD_SIZE
    for at in range(receivers):
        for a in range(2):
            columns = slice((2 * at + a) * HEAD_SIZE, (2 * at + a + 1) * HEAD_SIZE)
            core, group = at % CORES, at // CORES
            out_ref[core, group, a * PIECE : (a + 1) * PIECE, :] = query_ref[:, columns]
            out_ref[core, group, (2 + a) * PIECE : (3 + a) * PIECE, :] = grad_ref[:, columns]
    product = grad_ref[...].astype(f32) * row_ref[...].astype(f32)
    product_high = product.astype(bf16)
    product_low = (product - product_high.astype(f32)).astype(bf16)
    which = lax.broadcasted_iota(jnp.int32, (heads, width), 1) // HEAD_SIZE
    member = jnp.where(which == lax.broadcasted_iota(jnp.int32, (heads, width), 0), 1.0, 0.0).astype(bf16)
    delta = dot_t(member, product_high) + dot_t(member, product_low)
    parts = three_parts(lse_ref[...]) + three_parts(delta)
    rows = jnp.concatenate([p.astype(f32) for p in parts], axis=0)
    rows = jnp.concatenate([rows, rows], axis=1)
    lane = lax.broadcasted_iota(jnp.int32, rows.shape, 1) // PIECE
    rows = jnp.where(lane == parity_ref[0], rows, 0.0).astype(bf16)
    total = receivers * META_ROWS
    row_at = lax.broadcasted_iota(jnp.int32, (total, 6 * heads), 0)
    column_at = lax.broadcasted_iota(jnp.int32, (total, 6 * heads), 1)
    receiver = (row_at // META_ROWS) % groups * CORES + row_at // (META_ROWS * groups)
    t = row_at % META_ROWS
    source = ((t // 6) * 3 + t % 3) * heads + 2 * receiver + (t // 3) % 2
    pick = jnp.where((t < 12) & (column_at == source), 1.0, 0.0).astype(bf16)
    meta = dot_n(pick, rows).astype(bf16)
    out_ref[:, :, 4 * PIECE : 4 * PIECE + META_ROWS, :] = meta.reshape(CORES, groups, META_ROWS, HEAD_SIZE)


def pack_queries(parity, queries, grads, rows, lse, groups, steps=4):
    width = queries.shape[1] // steps
    height = 4 * PIECE + META_ROWS
    return pl.pallas_call(
        pack_queries_kernel,
        grid=(steps,),
        in_specs=[pl.BlockSpec(memory_space=pltpu.SMEM)]
        + [pl.BlockSpec((PIECE, width), lambda i: (0, i))] * 3
        + [pl.BlockSpec((lse.shape[0] // steps, PIECE), lambda i: (i, 0))],
        out_specs=pl.BlockSpec((CORES, groups // steps, height, HEAD_SIZE), lambda i: (0, i, 0, 0)),
        out_shape=jax.ShapeDtypeStruct((CORES, groups, height, HEAD_SIZE), bf16),
        name="pack_queries",
    )(parity, queries, grads, rows, lse)


def sweep(strips, causal, key_base, kv_ref, q_ref, lo_ref, dk_ref, dv_ref, dq_ref, part_ref):
    pieces = CHUNK // PIECE
    base = strips[0][1]
    for n, (at, first, last) in enumerate(strips):
        strip = slice((first - base) * CHUNK, (last - base) * CHUNK)
        height = (last - first) * CHUNK
        sources = slice(first * pieces, last * pieces)
        key = kv_ref[sources, 0:PIECE, :].reshape(height, HEAD_SIZE)
        value = kv_ref[sources, PIECE : 2 * PIECE, :].reshape(height, HEAD_SIZE)
        sources = slice(at * pieces, (at + 1) * pieces)

        def both(row):
            return jnp.concatenate(
                [q_ref[sources, (row + a) * PIECE : (row + a + 1) * PIECE, :].reshape(CHUNK, HEAD_SIZE) for a in range(2)]
            )

        query = both(0)
        grad = both(2)
        meta = q_ref[sources, 4 * PIECE : 4 * PIECE + META_ROWS, :].astype(f32)
        meta = meta[0] + meta[1]
        rows = [meta[3 * r : 3 * r + 1] + meta[3 * r + 1 : 3 * r + 2] + meta[3 * r + 2 : 3 * r + 3] for r in range(4)]
        lse = jnp.concatenate(rows[0:2], axis=1) * log2_e
        delta = jnp.concatenate(rows[2:4], axis=1)
        lo = lo_ref[at] - (key_base + first * CHUNK)
        lo = jnp.concatenate([lo, lo], axis=1)
        key_at = lax.broadcasted_iota(jnp.int32, (height, 2 * CHUNK), 0)
        allowed = key_at >= lo
        if causal:
            query_at = lax.broadcasted_iota(jnp.int32, (1, 2 * CHUNK), 1) % CHUNK + at * CHUNK
            allowed = allowed & (key_at <= query_at)
        scores = dot_t(key, query)
        prob = jnp.where(allowed, jnp.exp2(scores * (score_scale * log2_e) - lse), 0.0)
        prob_grad = dot_t(value, grad)
        score_grad = ((prob * score_scale) * (prob_grad - delta)).astype(bf16)
        dv = dot_n(prob.astype(bf16), grad)
        dk = dot_n(score_grad, query)
        if n == 0:
            dv_ref[strip, :] = dv
            dk_ref[strip, :] = dk
        else:
            dv_ref[strip, :] += dv
            dk_ref[strip, :] += dk
        dq = t_dot(score_grad, key)
        for a in range(2):
            mine = dq[a * CHUNK : (a + 1) * CHUNK]
            if part_ref is not None:
                mine = mine + part_ref[a, at * CHUNK : (at + 1) * CHUNK, :]
            dq_ref[a, at * CHUNK : (at + 1) * CHUNK, :] = mine


def cross_kernel(near, core_ref, kv_ref, q_ref, lo_ref, *refs):
    part_ref = None if near else refs[0]
    dq_ref, out_ref, dk_ref, dv_ref = refs[-4:]
    chunks = LOOKBACK_SPAN // CHUNK
    for block in range(CORES):

        @pl.when(core_ref[0] == (block if near else 1 - block))
        def _():
            start, end = block * chunks // CORES, (block + 1) * chunks // CORES
            sweep(
                [(at, max(at, start), end) for at in range(end)],
                False, 0, kv_ref, q_ref, lo_ref, dk_ref, dv_ref, dq_ref, part_ref,
            )
            rest = slice(end * CHUNK, LOOKBACK_SPAN)
            if end < chunks:
                dq_ref[:, rest, :] = jnp.zeros_like(dq_ref[:, rest, :]) if near else part_ref[:, rest, :]
            out_ref[0] = dk_ref[...].astype(bf16)
            out_ref[1] = dv_ref[...].astype(bf16)


def own_kernel(kv_ref, q_ref, lo_ref, part_ref, out_ref, dk_ref, dv_ref, dq_ref):
    chunks = LOOKBACK_SPAN // CHUNK
    sweep(
        [(at, 0, at + 1) for at in range(chunks - 1, -1, -1)],
        True, LOOKBACK_SPAN, kv_ref, q_ref, lo_ref, dk_ref, dv_ref, dq_ref, part_ref,
    )
    for core in range(CORES):
        block = slice(core * HALF, (core + 1) * HALF)
        out_ref[core, 0] = dq_ref[0, block, :].astype(bf16)
        out_ref[core, 1] = dq_ref[1, block, :].astype(bf16)
        out_ref[core, 2] = dk_ref[block, :].astype(bf16)
        out_ref[core, 3] = dv_ref[block, :].astype(bf16)


def vmem_spec():
    return pl.BlockSpec(memory_space=pltpu.VMEM)


def smem_spec():
    return pl.BlockSpec(memory_space=pltpu.SMEM)


HALF = LOOKBACK_SPAN // CORES


def rows_scratch(rows):
    return [pltpu.VMEM((rows, HEAD_SIZE), f32)] * 2


def cost():
    pairs = LOOKBACK_SPAN * LOOKBACK_SPAN
    return pl.CostEstimate(flops=pairs * 5 * 2 * HEAD_SIZE, transcendentals=pairs, bytes_accessed=4 << 20)


def cross_terms(near, core, kv, q, lo, *part):
    return pl.pallas_call(
        functools.partial(cross_kernel, near),
        in_specs=[smem_spec()] + [vmem_spec()] * (3 + len(part)),
        out_specs=[vmem_spec()] * 2,
        out_shape=[
            jax.ShapeDtypeStruct((2, LOOKBACK_SPAN, HEAD_SIZE), f32),
            jax.ShapeDtypeStruct((2, HALF, HEAD_SIZE), bf16),
        ],
        scratch_shapes=rows_scratch(HALF),
        compiler_params=pltpu.CompilerParams(vmem_limit_bytes=40 << 20),
        cost_estimate=cost(),
        name="cross_near" if near else "cross_far",
    )(core, kv, q, lo, *part)


def own_terms(kv, q, lo, part):
    return pl.pallas_call(
        own_kernel,
        in_specs=[vmem_spec()] * 4,
        out_specs=vmem_spec(),
        out_shape=jax.ShapeDtypeStruct((CORES, 4, HALF, HEAD_SIZE), bf16),
        scratch_shapes=rows_scratch(LOOKBACK_SPAN) + [pltpu.VMEM((2, LOOKBACK_SPAN, HEAD_SIZE), f32)],
        compiler_params=pltpu.CompilerParams(vmem_limit_bytes=40 << 20),
        cost_estimate=cost(),
        name="own_terms",
    )(kv, q, lo, part)


def join_kernel(near, core_ref, own_ref, back_ref, *refs):
    dk_ref, dv_ref = refs[-2:]
    for k in range(CORES):

        @pl.when(core_ref[0] == (k if near else 1 - k))
        def _():
            columns = slice(k * HEAD_SIZE, (k + 1) * HEAD_SIZE)
            for i, out_ref in enumerate((dk_ref, dv_ref)):
                if not near:
                    others = slice((1 - k) * HEAD_SIZE, (2 - k) * HEAD_SIZE)
                    out_ref[:, others] = refs[i][:, others]
                out_ref[:, columns] = (own_ref[k, 2 + i].astype(f32) + back_ref[i].astype(f32)).astype(bf16)


def join(near, core, own, back, *halves):
    return pl.pallas_call(
        functools.partial(join_kernel, near),
        in_specs=[smem_spec()] + [vmem_spec()] * (2 + len(halves)),
        out_specs=[vmem_spec()] * 2,
        out_shape=[jax.ShapeDtypeStruct((HALF, 2 * HEAD_SIZE), bf16)] * 2,
        compiler_params=pltpu.CompilerParams(vmem_limit_bytes=16 << 20),
        name="join_near" if near else "join_far",
    )(core, own, back, *halves)


def join_queries_kernel(own_ref, dq_ref):
    for core in range(CORES):
        for a in range(2):
            at = 2 * core + a
            dq_ref[:, at * HEAD_SIZE : (at + 1) * HEAD_SIZE] = own_ref[core, a]


def join_queries(own):
    return pl.pallas_call(
        join_queries_kernel,
        in_specs=[vmem_spec()],
        out_specs=vmem_spec(),
        out_shape=jax.ShapeDtypeStruct((HALF, 4 * HEAD_SIZE), bf16),
        compiler_params=pltpu.CompilerParams(vmem_limit_bytes=16 << 20),
        name="join_queries",
    )(own)


def first_allowed(doc_ids, chip):
    padded = jnp.concatenate([jnp.full((LOOKBACK_SPAN,), -1, jnp.int32), doc_ids])
    window = lax.dynamic_slice_in_dim(padded, chip * LOOKBACK_SPAN, 2 * LOOKBACK_SPAN, 0)
    own = window[LOOKBACK_SPAN:]
    document_start = jnp.sum((window[:, None] < own[None, :]).astype(jnp.int32), axis=0)
    reach_start = jnp.arange(1, LOOKBACK_SPAN + 1, dtype=jnp.int32)
    return jnp.maximum(document_start, reach_start).reshape(LOOKBACK_SPAN // CHUNK, 1, CHUNK)


def exchange(value):
    value = value.reshape((-1,) + value.shape[2:])
    return lax.all_to_all(value, ("core", "head"), split_axis=0, concat_axis=0, tiled=True)


def on_device(queries, keys, values, rows, grads, lse, doc_ids):
    chips = lax.axis_size("chip")
    groups = lax.axis_size("head")
    chip = lax.axis_index("chip")
    core = lax.axis_index("core").astype(jnp.int32).reshape(1)
    parity = (lax.axis_index("head") % 2).astype(jnp.int32).reshape(1)
    lo = first_allowed(doc_ids, chip)
    kv = exchange(pack_keys(keys, values, groups))
    packed = pack_queries(parity, queries, grads, rows, lse, groups)
    kv, packed = lax.optimization_barrier((kv, packed))
    q = exchange(packed)
    kv_before = lax.ppermute(kv, "chip", [(c, c + 1) for c in range(chips - 1)])
    dq_part, near = cross_terms(True, core, kv_before, q, lo)
    back_near = lax.ppermute(near, "chip", [(c + 1, c) for c in range(chips - 1)])
    dq_part, far = cross_terms(False, core, kv_before, q, lo, dq_part)
    back_far = lax.ppermute(
        far,
        ("chip", "core"),
        [(CORES * (c + 1) + k, CORES * c + 1 - k) for c in range(chips - 1) for k in range(CORES)],
    )
    own = own_terms(kv, q, lo, dq_part)
    own = lax.all_to_all(own, "core", split_axis=0, concat_axis=0, tiled=True)
    query_grad = join_queries(own)
    halves = join(True, core, own, back_near)
    key_grad, value_grad = join(False, core, own, back_far, *halves)
    return query_grad, key_grad, value_grad


def solution(mesh):
    seq, head = mesh.devices.shape
    fine = Mesh(mesh.devices.reshape(seq // CORES, CORES, head), ("chip", "core", "head"))
    tokens = ("chip", "core", "head")
    return jax.shard_map(
        on_device,
        mesh=fine,
        in_specs=(P(tokens), P(tokens), P(tokens), P(tokens), P(tokens), P(None, tokens), P()),
        out_specs=(P(("chip", "core"), "head"),) * 3,
        check_vma=False,
    )
```

```python
import functools
import math

import jax
import jax.numpy as jnp
from jax import lax
from jax.experimental import pallas as pl
from jax.experimental.pallas import tpu as pltpu
from jax.sharding import Mesh
from jax.sharding import PartitionSpec as P

HEAD_SIZE = 128
LOOKBACK_SPAN = 1024
CORES = 2
PIECE = 64
META_ROWS = 8
CHUNK = 128

score_scale = 168.0 ** (-0.5)
log2_e = math.log2(math.e)

f32 = jnp.float32
bf16 = jnp.bfloat16


def dot_t(left, right):
    return lax.dot_general(left, right, (((1,), (1,)), ((), ())), preferred_element_type=f32)


def dot_n(left, right):
    return lax.dot_general(left, right, (((1,), (0,)), ((), ())), preferred_element_type=f32)


def t_dot(left, right):
    return lax.dot_general(left, right, (((0,), (0,)), ((), ())), preferred_element_type=f32)


def pack_keys_kernel(key_ref, value_ref, out_ref):
    for at in range(out_ref.shape[0]):
        columns = slice(at * HEAD_SIZE, (at + 1) * HEAD_SIZE)
        out_ref[at, 0:PIECE, :] = key_ref[:, columns]
        out_ref[at, PIECE : 2 * PIECE, :] = value_ref[:, columns]


def pack_keys(keys, values, steps=2):
    heads = keys.shape[1] // HEAD_SIZE
    return pl.pallas_call(
        pack_keys_kernel,
        grid=(steps,),
        in_specs=[pl.BlockSpec((PIECE, keys.shape[1] // steps), lambda i: (0, i))] * 2,
        out_specs=pl.BlockSpec((heads // steps, 2 * PIECE, HEAD_SIZE), lambda i: (i, 0, 0)),
        out_shape=jax.ShapeDtypeStruct((heads, 2 * PIECE, HEAD_SIZE), bf16),
        name="pack_keys",
    )(keys, values)


def three_parts(value):
    high = value.astype(bf16)
    rest = value - high.astype(f32)
    middle = rest.astype(bf16)
    return [high, middle, (rest - middle.astype(f32)).astype(bf16)]


def pack_queries_kernel(core_ref, query_ref, grad_ref, row_ref, lse_ref, keep_ref, give_ref):
    groups = keep_ref.shape[0]
    heads = 2 * CORES * groups
    width = heads * HEAD_SIZE
    for core in range(CORES):

        @pl.when(core_ref[0] == core)
        def _():
            for out_ref, to in ((keep_ref, core), (give_ref, 1 - core)):
                for group in range(groups):
                    for a in range(2):
                        head = 2 * (CORES * group + to) + a
                        columns = slice(head * HEAD_SIZE, (head + 1) * HEAD_SIZE)
                        out_ref[group, a * PIECE : (a + 1) * PIECE, :] = query_ref[:, columns]
                        out_ref[group, (2 + a) * PIECE : (3 + a) * PIECE, :] = grad_ref[:, columns]

    product = grad_ref[...].astype(f32) * row_ref[...].astype(f32)
    product_high = product.astype(bf16)
    product_low = (product - product_high.astype(f32)).astype(bf16)
    which = lax.broadcasted_iota(jnp.int32, (heads, width), 1) // HEAD_SIZE
    member = jnp.where(which == lax.broadcasted_iota(jnp.int32, (heads, width), 0), 1.0, 0.0).astype(bf16)
    delta = dot_t(member, product_high) + dot_t(member, product_low)
    parts = three_parts(lse_ref[...]) + three_parts(delta)
    rows = jnp.concatenate([p.astype(f32) for p in parts], axis=0).astype(bf16)
    total = groups * META_ROWS
    row_at = lax.broadcasted_iota(jnp.int32, (total, 6 * heads), 0)
    column_at = lax.broadcasted_iota(jnp.int32, (total, 6 * heads), 1)
    for out_ref, to in ((keep_ref, core_ref[0]), (give_ref, 1 - core_ref[0])):
        first_head = 2 * (CORES * (row_at // META_ROWS) + to)
        halves = []
        for half in range(2):
            m = 2 * (row_at % META_ROWS) + half
            source = ((m // 6) * 3 + m % 3) * heads + first_head + (m // 3) % 2
            pick = jnp.where((m < 12) & (column_at == source), 1.0, 0.0).astype(bf16)
            halves.append(dot_n(pick, rows))
        meta = jnp.concatenate(halves, axis=1).reshape(groups, META_ROWS, HEAD_SIZE)
        for group in range(groups):
            out_ref[group, 4 * PIECE : 4 * PIECE + META_ROWS, :] = meta[group].astype(bf16)


def pack_queries(core, queries, grads, rows, lse, groups, steps=4):
    width = queries.shape[1] // steps
    height = 4 * PIECE + META_ROWS
    return pl.pallas_call(
        pack_queries_kernel,
        grid=(steps,),
        in_specs=[pl.BlockSpec(memory_space=pltpu.SMEM)]
        + [pl.BlockSpec((PIECE, width), lambda i: (0, i))] * 3
        + [pl.BlockSpec((lse.shape[0] // steps, PIECE), lambda i: (i, 0))],
        out_specs=[pl.BlockSpec((groups // steps, height, HEAD_SIZE), lambda i: (i, 0, 0))] * 2,
        out_shape=[jax.ShapeDtypeStruct((groups, height, HEAD_SIZE), bf16)] * 2,
        name="pack_queries",
    )(core, queries, grads, rows, lse)


def chunk_rows(ref, slots, first, last, row):
    per_block = LOOKBACK_SPAN // CORES // CHUNK
    pieces = CHUNK // PIECE
    found = []
    for block in range(CORES):
        start, end = max(first, block * per_block), min(last, (block + 1) * per_block)
        if start < end:
            at = slice((start - block * per_block) * pieces, (end - block * per_block) * pieces)
            rows = ref[at, slots[block], row : row + PIECE, :]
            found.append(rows.reshape((end - start) * CHUNK, HEAD_SIZE))
    return found[0] if len(found) == 1 else jnp.concatenate(found)


def chunk_meta(ref, slots, at):
    per_block = LOOKBACK_SPAN // CORES // CHUNK
    piece = (at % per_block) * (CHUNK // PIECE)
    meta = [
        ref[piece + i, slots[at // per_block], 4 * PIECE : 4 * PIECE + META_ROWS, :].astype(f32) for i in range(2)
    ]
    turned = [pltpu.roll(m, PIECE, 1) for m in meta]
    left = lax.broadcasted_iota(jnp.int32, meta[0].shape, 1) < PIECE
    halves = (jnp.where(left, meta[0], turned[1]), jnp.where(left, turned[0], meta[1]))
    pieces = [halves[m % 2][m // 2 : m // 2 + 1] for m in range(12)]
    rows = [pieces[3 * r] + pieces[3 * r + 1] + pieces[3 * r + 2] for r in range(4)]
    return jnp.concatenate(rows[0:2], axis=1), jnp.concatenate(rows[2:4], axis=1)


def sweep(strips, causal, key_base, key_slots, q_slots, kv_ref, q_ref, lo_ref, dk_ref, dv_ref, dq_ref, part_ref):
    base = strips[0][1]
    for n, (at, first, last) in enumerate(strips):
        strip = slice((first - base) * CHUNK, (last - base) * CHUNK)
        height = (last - first) * CHUNK
        key = chunk_rows(kv_ref, key_slots, first, last, 0)
        value = chunk_rows(kv_ref, key_slots, first, last, PIECE)
        query, grad = [
            jnp.concatenate([chunk_rows(q_ref, q_slots, at, at + 1, (row + a) * PIECE) for a in range(2)])
            for row in (0, 2)
        ]
        lse, delta = chunk_meta(q_ref, q_slots, at)
        lse = lse * log2_e
        lo = lo_ref[at] - (key_base + first * CHUNK)
        lo = jnp.concatenate([lo, lo], axis=1)
        key_at = lax.broadcasted_iota(jnp.int32, (height, 2 * CHUNK), 0)
        allowed = key_at >= lo
        if causal:
            query_at = lax.broadcasted_iota(jnp.int32, (1, 2 * CHUNK), 1) % CHUNK + at * CHUNK
            allowed = allowed & (key_at <= query_at)
        scores = dot_t(key, query)
        prob = jnp.where(allowed, jnp.exp2(scores * (score_scale * log2_e) - lse), 0.0)
        prob_grad = dot_t(value, grad)
        score_grad = ((prob * score_scale) * (prob_grad - delta)).astype(bf16)
        dv = dot_n(prob.astype(bf16), grad)
        dk = dot_n(score_grad, query)
        if n == 0:
            dv_ref[strip, :] = dv
            dk_ref[strip, :] = dk
        else:
            dv_ref[strip, :] += dv
            dk_ref[strip, :] += dk
        dq = t_dot(score_grad, key)
        for a in range(2):
            mine = dq[a * CHUNK : (a + 1) * CHUNK]
            if part_ref is not None:
                mine = mine + part_ref[a, at * CHUNK : (at + 1) * CHUNK, :]
            dq_ref[a, at * CHUNK : (at + 1) * CHUNK, :] = mine


def cross_kernel(near, core_ref, kv_ref, q_ref, lo_ref, *refs):
    part_ref = None if near else refs[0]
    dq_ref, out_ref, dk_ref, dv_ref = refs[-4:]
    chunks = LOOKBACK_SPAN // CHUNK
    for block in range(CORES):
        core = block if near else 1 - block

        @pl.when(core_ref[0] == core)
        def _():
            start, end = block * chunks // CORES, (block + 1) * chunks // CORES
            sweep(
                [(at, max(at, start), end) for at in range(end)],
                False, 0, (0, 0), (core, 1 - core), kv_ref, q_ref, lo_ref, dk_ref, dv_ref, dq_ref, part_ref,
            )
            rest = slice(end * CHUNK, LOOKBACK_SPAN)
            if end < chunks:
                dq_ref[:, rest, :] = jnp.zeros_like(dq_ref[:, rest, :]) if near else part_ref[:, rest, :]
            out_ref[0] = dk_ref[...].astype(bf16)
            out_ref[1] = dv_ref[...].astype(bf16)


def own_kernel(core_ref, kv_near_ref, kv_far_ref, q_ref, lo_ref, part_ref, out_ref, dk_ref, dv_ref, dq_ref, kv_ref):
    kv_ref[:, 0] = kv_near_ref[...]
    kv_ref[:, 1] = kv_far_ref[...]
    chunks = LOOKBACK_SPAN // CHUNK
    slots = (core_ref[0], 1 - core_ref[0])
    sweep(
        [(at, 0, at + 1) for at in range(chunks - 1, -1, -1)],
        True, LOOKBACK_SPAN, slots, slots, kv_ref, q_ref, lo_ref, dk_ref, dv_ref, dq_ref, part_ref,
    )
    for core in range(CORES):
        block = slice(core * HALF, (core + 1) * HALF)
        out_ref[core, 0] = dq_ref[0, block, :].astype(bf16)
        out_ref[core, 1] = dq_ref[1, block, :].astype(bf16)
        out_ref[core, 2] = dk_ref[block, :].astype(bf16)
        out_ref[core, 3] = dv_ref[block, :].astype(bf16)


def vmem_spec():
    return pl.BlockSpec(memory_space=pltpu.VMEM)


def smem_spec():
    return pl.BlockSpec(memory_space=pltpu.SMEM)


HALF = LOOKBACK_SPAN // CORES


def rows_scratch(rows):
    return [pltpu.VMEM((rows, HEAD_SIZE), f32)] * 2


def cost():
    pairs = LOOKBACK_SPAN * LOOKBACK_SPAN
    return pl.CostEstimate(flops=pairs * 5 * 2 * HEAD_SIZE, transcendentals=pairs, bytes_accessed=4 << 20)


def cross_terms(near, core, kv, q, lo, *part):
    return pl.pallas_call(
        functools.partial(cross_kernel, near),
        in_specs=[smem_spec()] + [vmem_spec()] * (3 + len(part)),
        out_specs=[vmem_spec()] * 2,
        out_shape=[
            jax.ShapeDtypeStruct((2, LOOKBACK_SPAN, HEAD_SIZE), f32),
            jax.ShapeDtypeStruct((2, HALF, HEAD_SIZE), bf16),
        ],
        scratch_shapes=rows_scratch(HALF),
        compiler_params=pltpu.CompilerParams(vmem_limit_bytes=40 << 20),
        cost_estimate=cost(),
        name="cross_near" if near else "cross_far",
    )(core, kv, q, lo, *part)


def own_terms(core, kv_near, kv_far, q, lo, part):
    return pl.pallas_call(
        own_kernel,
        in_specs=[smem_spec()] + [vmem_spec()] * 5,
        out_specs=vmem_spec(),
        out_shape=jax.ShapeDtypeStruct((CORES, 4, HALF, HEAD_SIZE), bf16),
        scratch_shapes=rows_scratch(LOOKBACK_SPAN)
        + [
            pltpu.VMEM((2, LOOKBACK_SPAN, HEAD_SIZE), f32),
            pltpu.VMEM((HALF // PIECE, CORES, 2 * PIECE, HEAD_SIZE), bf16),
        ],
        compiler_params=pltpu.CompilerParams(vmem_limit_bytes=40 << 20),
        cost_estimate=cost(),
        name="own_terms",
    )(core, kv_near, kv_far, q, lo, part)


def join_kernel(near, core_ref, own_ref, back_ref, *refs):
    dk_ref, dv_ref = refs[-2:]
    if near:
        dq_ref = refs[0]
        for core in range(CORES):
            for a in range(2):
                at = 2 * core + a
                dq_ref[:, at * HEAD_SIZE : (at + 1) * HEAD_SIZE] = own_ref[core, a]
    for k in range(CORES):

        @pl.when(core_ref[0] == (k if near else 1 - k))
        def _():
            columns = slice(k * HEAD_SIZE, (k + 1) * HEAD_SIZE)
            for i, out_ref in enumerate((dk_ref, dv_ref)):
                if not near:
                    others = slice((1 - k) * HEAD_SIZE, (2 - k) * HEAD_SIZE)
                    out_ref[:, others] = refs[i][:, others]
                out_ref[:, columns] = (own_ref[k, 2 + i].astype(f32) + back_ref[i].astype(f32)).astype(bf16)


def join(near, core, own, back, *halves):
    shapes = [jax.ShapeDtypeStruct((HALF, 2 * HEAD_SIZE), bf16)] * 2
    if near:
        shapes = [jax.ShapeDtypeStruct((HALF, 4 * HEAD_SIZE), bf16)] + shapes
    return pl.pallas_call(
        functools.partial(join_kernel, near),
        in_specs=[smem_spec()] + [vmem_spec()] * (2 + len(halves)),
        out_specs=[vmem_spec()] * len(shapes),
        out_shape=shapes,
        compiler_params=pltpu.CompilerParams(vmem_limit_bytes=16 << 20),
        name="join_near" if near else "join_far",
    )(core, own, back, *halves)


def first_allowed(doc_ids, chip):
    padded = jnp.concatenate([jnp.full((LOOKBACK_SPAN,), -1, jnp.int32), doc_ids])
    window = lax.dynamic_slice_in_dim(padded, chip * LOOKBACK_SPAN, 2 * LOOKBACK_SPAN, 0)
    own = window[LOOKBACK_SPAN:]
    document_start = jnp.sum((window[:, None] < own[None, :]).astype(jnp.int32), axis=0)
    reach_start = jnp.arange(1, LOOKBACK_SPAN + 1, dtype=jnp.int32)
    return jnp.maximum(document_start, reach_start).reshape(LOOKBACK_SPAN // CHUNK, 1, CHUNK)


def exchange(value):
    return lax.all_to_all(value, "head", split_axis=0, concat_axis=0, tiled=True)


def other_core(value):
    return lax.ppermute(value, "core", [(0, 1), (1, 0)])


def next_chip(value, step, cross):
    chips = lax.axis_size("chip")
    pairs = [
        (CORES * c + k, CORES * (c + step) + (1 - k if cross else k))
        for c in range(max(0, -step), min(chips, chips - step))
        for k in range(CORES)
    ]
    return lax.ppermute(value, ("chip", "core"), pairs)


def on_device(queries, keys, values, rows, grads, lse, doc_ids):
    groups = lax.axis_size("head")
    chip = lax.axis_index("chip")
    core_at = lax.axis_index("core").astype(jnp.int32)
    core = core_at.reshape(1)
    lo = first_allowed(doc_ids, chip)
    kv = exchange(pack_keys(keys, values).reshape(groups, CORES, 2 * PIECE, HEAD_SIZE))
    keep, give = pack_queries(core, queries, grads, rows, lse, groups)
    packed = jnp.stack([keep, other_core(give)], axis=1)
    kv, packed = lax.optimization_barrier((kv, packed))
    q = exchange(packed)
    kv_mine = jnp.where(core_at == 0, kv[:, 0], kv[:, 1])
    kv_other = jnp.where(core_at == 0, kv[:, 1], kv[:, 0])
    before_near = next_chip(kv_mine, 1, False)[:, None]
    before_far = next_chip(kv_other, 1, True)[:, None]
    kv_far = other_core(kv_other)
    dq_part, near = cross_terms(True, core, before_near, q, lo)
    back_near = next_chip(near, -1, False)
    dq_part, far = cross_terms(False, core, before_far, q, lo, dq_part)
    back_far = next_chip(far, -1, True)
    own = own_terms(core, kv_mine, kv_far, q, lo, dq_part)
    own = lax.all_to_all(own, "core", split_axis=0, concat_axis=0, tiled=True)
    query_grad, *halves = join(True, core, own, back_near)
    key_grad, value_grad = join(False, core, own, back_far, *halves)
    return query_grad, key_grad, value_grad


def solution(mesh):
    seq, head = mesh.devices.shape
    fine = Mesh(mesh.devices.reshape(seq // CORES, CORES, head), ("chip", "core", "head"))
    tokens = ("chip", "core", "head")
    return jax.shard_map(
        on_device,
        mesh=fine,
        in_specs=(P(tokens), P(tokens), P(tokens), P(tokens), P(tokens), P(None, tokens), P()),
        out_specs=(P(("chip", "core"), "head"),) * 3,
        check_vma=False,
    )
```

```python
import math

import jax
import jax.numpy as jnp
from jax import lax
from jax.experimental import pallas as pl
from jax.experimental.pallas import tpu as pltpu
from jax.sharding import Mesh
from jax.sharding import PartitionSpec as P

HEAD_SIZE = 128
LOOKBACK_SPAN = 1024
CORES = 2
PIECE = 64
META_ROWS = 8
CHUNK = 128

score_scale = 168.0 ** (-0.5)
log2_e = math.log2(math.e)

f32 = jnp.float32
bf16 = jnp.bfloat16


def dot_t(left, right):
    return lax.dot_general(left, right, (((1,), (1,)), ((), ())), preferred_element_type=f32)


def dot_n(left, right):
    return lax.dot_general(left, right, (((1,), (0,)), ((), ())), preferred_element_type=f32)


def t_dot(left, right):
    return lax.dot_general(left, right, (((0,), (0,)), ((), ())), preferred_element_type=f32)


def pack_keys_kernel(key_ref, value_ref, out_ref):
    for at in range(CORES * out_ref.shape[1]):
        columns = slice(at * HEAD_SIZE, (at + 1) * HEAD_SIZE)
        out_ref[at % CORES, at // CORES, 0:PIECE, :] = key_ref[:, columns]
        out_ref[at % CORES, at // CORES, PIECE : 2 * PIECE, :] = value_ref[:, columns]


def pack_keys(keys, values, groups, steps=2):
    width = keys.shape[1] // steps
    return pl.pallas_call(
        pack_keys_kernel,
        grid=(steps,),
        in_specs=[pl.BlockSpec((PIECE, width), lambda i: (0, i))] * 2,
        out_specs=pl.BlockSpec((CORES, groups // steps, 2 * PIECE, HEAD_SIZE), lambda i: (0, i, 0, 0)),
        out_shape=jax.ShapeDtypeStruct((CORES, groups, 2 * PIECE, HEAD_SIZE), bf16),
        name="pack_keys",
    )(keys, values)


def three_parts(value):
    high = value.astype(bf16)
    rest = value - high.astype(f32)
    middle = rest.astype(bf16)
    return [high, middle, (rest - middle.astype(f32)).astype(bf16)]


def pack_queries_kernel(query_ref, grad_ref, row_ref, lse_ref, out_ref):
    groups = out_ref.shape[1]
    receivers = CORES * groups
    heads = 2 * receivers
    width = heads * HEAD_SIZE
    for at in range(receivers):
        for a in range(2):
            columns = slice((2 * at + a) * HEAD_SIZE, (2 * at + a + 1) * HEAD_SIZE)
            core, group = at % CORES, at // CORES
            out_ref[core, group, a * PIECE : (a + 1) * PIECE, :] = query_ref[:, columns]
            out_ref[core, group, (2 + a) * PIECE : (3 + a) * PIECE, :] = grad_ref[:, columns]
    product = grad_ref[...].astype(f32) * row_ref[...].astype(f32)
    product_high = product.astype(bf16)
    product_low = (product - product_high.astype(f32)).astype(bf16)
    which = lax.broadcasted_iota(jnp.int32, (heads, width), 1) // HEAD_SIZE
    member = jnp.where(which == lax.broadcasted_iota(jnp.int32, (heads, width), 0), 1.0, 0.0).astype(bf16)
    delta = dot_t(member, product_high) + dot_t(member, product_low)
    parts = three_parts(lse_ref[...]) + three_parts(delta)
    rows = jnp.concatenate([p.astype(f32) for p in parts], axis=0).astype(bf16)
    total = receivers * META_ROWS
    row_at = lax.broadcasted_iota(jnp.int32, (total, 6 * heads), 0)
    column_at = lax.broadcasted_iota(jnp.int32, (total, 6 * heads), 1)
    receiver = (row_at // META_ROWS) % groups * CORES + row_at // (META_ROWS * groups)
    halves = []
    for half in range(2):
        m = 2 * (row_at % META_ROWS) + half
        source = ((m // 6) * 3 + m % 3) * heads + 2 * receiver + (m // 3) % 2
        pick = jnp.where((m < 12) & (column_at == source), 1.0, 0.0).astype(bf16)
        halves.append(dot_n(pick, rows))
    meta = jnp.concatenate(halves, axis=1).reshape(CORES, groups, META_ROWS, HEAD_SIZE)
    for core in range(CORES):
        for group in range(groups):
            out_ref[core, group, 4 * PIECE : 4 * PIECE + META_ROWS, :] = meta[core, group].astype(bf16)


def pack_queries(queries, grads, rows, lse, groups, steps=4):
    width = queries.shape[1] // steps
    height = 4 * PIECE + META_ROWS
    return pl.pallas_call(
        pack_queries_kernel,
        grid=(steps,),
        in_specs=[pl.BlockSpec((PIECE, width), lambda i: (0, i))] * 3
        + [pl.BlockSpec((lse.shape[0] // steps, PIECE), lambda i: (i, 0))],
        out_specs=pl.BlockSpec((CORES, groups // steps, height, HEAD_SIZE), lambda i: (0, i, 0, 0)),
        out_shape=jax.ShapeDtypeStruct((CORES, groups, height, HEAD_SIZE), bf16),
        name="pack_queries",
    )(queries, grads, rows, lse)


def chunk_meta(ref, at):
    meta = [ref[2 * at + i, 4 * PIECE : 4 * PIECE + META_ROWS, :].astype(f32) for i in range(2)]
    turned = [pltpu.roll(m, PIECE, 1) for m in meta]
    left = lax.broadcasted_iota(jnp.int32, meta[0].shape, 1) < PIECE
    halves = (jnp.where(left, meta[0], turned[1]), jnp.where(left, turned[0], meta[1]))
    pieces = [halves[m % 2][m // 2 : m // 2 + 1] for m in range(12)]
    rows = [pieces[3 * r] + pieces[3 * r + 1] + pieces[3 * r + 2] for r in range(4)]
    return jnp.concatenate(rows[0:2], axis=1), jnp.concatenate(rows[2:4], axis=1)


def sweep(causal, key_base, kv_ref, q_ref, lo_ref, dk_ref, dv_ref, dq_ref, part_ref):
    pieces = CHUNK // PIECE
    chunks = LOOKBACK_SPAN // CHUNK
    order = range(chunks - 1, -1, -1) if causal else range(chunks)
    for n, at in enumerate(order):
        first, last = (0, at + 1) if causal else (at, chunks)
        strip = slice(first * CHUNK, last * CHUNK)
        height = (last - first) * CHUNK
        sources = slice(first * pieces, last * pieces)
        key = kv_ref[sources, 0:PIECE, :].reshape(height, HEAD_SIZE)
        value = kv_ref[sources, PIECE : 2 * PIECE, :].reshape(height, HEAD_SIZE)
        sources = slice(at * pieces, (at + 1) * pieces)

        def both(row):
            return jnp.concatenate(
                [q_ref[sources, (row + a) * PIECE : (row + a + 1) * PIECE, :].reshape(CHUNK, HEAD_SIZE) for a in range(2)]
            )

        query = both(0)
        grad = both(2)
        lse, delta = chunk_meta(q_ref, at)
        lse = lse * log2_e
        lo = lo_ref[at] - (key_base + first * CHUNK)
        lo = jnp.concatenate([lo, lo], axis=1)
        key_at = lax.broadcasted_iota(jnp.int32, (height, 2 * CHUNK), 0)
        allowed = key_at >= lo
        if causal:
            query_at = lax.broadcasted_iota(jnp.int32, (1, 2 * CHUNK), 1) % CHUNK + at * CHUNK
            allowed = allowed & (key_at <= query_at)
        scores = dot_t(key, query)
        prob = jnp.where(allowed, jnp.exp2(scores * (score_scale * log2_e) - lse), 0.0)
        prob_grad = dot_t(value, grad)
        score_grad = ((prob * score_scale) * (prob_grad - delta)).astype(bf16)
        dv = dot_n(prob.astype(bf16), grad)
        dk = dot_n(score_grad, query)
        if n == 0:
            dv_ref[strip, :] = dv
            dk_ref[strip, :] = dk
        else:
            dv_ref[strip, :] += dv
            dk_ref[strip, :] += dk
        dq = t_dot(score_grad, key)
        for a in range(2):
            mine = dq[a * CHUNK : (a + 1) * CHUNK]
            if part_ref is not None:
                mine = mine + part_ref[a, at * CHUNK : (at + 1) * CHUNK, :]
            dq_ref[a, at * CHUNK : (at + 1) * CHUNK, :] = mine


def cross_kernel(core_ref, kv_ref, q_ref, lo_ref, dq_ref, near_ref, far_ref, dk_ref, dv_ref):
    sweep(False, 0, kv_ref, q_ref, lo_ref, dk_ref, dv_ref, dq_ref, None)
    half = LOOKBACK_SPAN // CORES
    near = pl.ds(pl.multiple_of(core_ref[0] * half, half), half)
    far = pl.ds(pl.multiple_of((1 - core_ref[0]) * half, half), half)
    near_ref[0] = dk_ref[near, :].astype(bf16)
    near_ref[1] = dv_ref[near, :].astype(bf16)
    far_ref[0] = dk_ref[far, :].astype(bf16)
    far_ref[1] = dv_ref[far, :].astype(bf16)


def own_kernel(core_ref, kv_ref, q_ref, lo_ref, part_ref, near_dq_ref, near_ref, far_ref, dk_ref, dv_ref, dq_ref):
    sweep(True, LOOKBACK_SPAN, kv_ref, q_ref, lo_ref, dk_ref, dv_ref, dq_ref, part_ref)
    near = pl.ds(pl.multiple_of(core_ref[0] * HALF, HALF), HALF)
    far = pl.ds(pl.multiple_of((1 - core_ref[0]) * HALF, HALF), HALF)
    for a in range(2):
        near_dq_ref[a] = dq_ref[a, near, :].astype(bf16)
        far_ref[a] = dq_ref[a, far, :].astype(bf16)
    near_ref[0] = dk_ref[near, :]
    near_ref[1] = dv_ref[near, :]
    far_ref[2] = dk_ref[far, :].astype(bf16)
    far_ref[3] = dv_ref[far, :].astype(bf16)


def vmem_spec():
    return pl.BlockSpec(memory_space=pltpu.VMEM)


def smem_spec():
    return pl.BlockSpec(memory_space=pltpu.SMEM)


SPAN_SCRATCH = [
    pltpu.VMEM((LOOKBACK_SPAN, HEAD_SIZE), f32),
    pltpu.VMEM((LOOKBACK_SPAN, HEAD_SIZE), f32),
]
HALF = LOOKBACK_SPAN // CORES


def cost():
    pairs = LOOKBACK_SPAN * LOOKBACK_SPAN
    return pl.CostEstimate(flops=pairs * 5 * 2 * HEAD_SIZE, transcendentals=pairs, bytes_accessed=4 << 20)


def cross_terms(core, kv, q, lo):
    return pl.pallas_call(
        cross_kernel,
        in_specs=[smem_spec()] + [vmem_spec()] * 3,
        out_specs=[vmem_spec()] * 3,
        out_shape=[
            jax.ShapeDtypeStruct((2, LOOKBACK_SPAN, HEAD_SIZE), f32),
            jax.ShapeDtypeStruct((2, HALF, HEAD_SIZE), bf16),
            jax.ShapeDtypeStruct((2, HALF, HEAD_SIZE), bf16),
        ],
        scratch_shapes=SPAN_SCRATCH,
        compiler_params=pltpu.CompilerParams(vmem_limit_bytes=40 << 20),
        cost_estimate=cost(),
        name="cross_terms",
    )(core, kv, q, lo)


def own_terms(core, kv, q, lo, part):
    return pl.pallas_call(
        own_kernel,
        in_specs=[smem_spec()] + [vmem_spec()] * 4,
        out_specs=[vmem_spec()] * 3,
        out_shape=[
            jax.ShapeDtypeStruct((2, HALF, HEAD_SIZE), bf16),
            jax.ShapeDtypeStruct((2, HALF, HEAD_SIZE), f32),
            jax.ShapeDtypeStruct((4, HALF, HEAD_SIZE), bf16),
        ],
        scratch_shapes=SPAN_SCRATCH + [pltpu.VMEM((2, LOOKBACK_SPAN, HEAD_SIZE), f32)],
        compiler_params=pltpu.CompilerParams(vmem_limit_bytes=40 << 20),
        cost_estimate=cost(),
        name="own_terms",
    )(core, kv, q, lo, part)


def join_near_kernel(core_ref, near_ref, back_ref, dk_ref, dv_ref):
    for core in range(CORES):

        @pl.when(core_ref[0] == core)
        def _():
            columns = slice(core * HEAD_SIZE, (core + 1) * HEAD_SIZE)
            for i, out_ref in enumerate((dk_ref, dv_ref)):
                out_ref[:, columns] = (near_ref[i] + back_ref[i].astype(f32)).astype(bf16)


def join_far_kernel(core_ref, near_dq_ref, swapped_ref, back_ref, near_dk_ref, near_dv_ref, dq_ref, dk_ref, dv_ref):
    for core in range(CORES):

        @pl.when(core_ref[0] == core)
        def _():
            for a in range(2):
                at = 2 * core + a
                dq_ref[:, at * HEAD_SIZE : (at + 1) * HEAD_SIZE] = near_dq_ref[a]
                at = 2 * (1 - core) + a
                dq_ref[:, at * HEAD_SIZE : (at + 1) * HEAD_SIZE] = swapped_ref[a]
            near = slice(core * HEAD_SIZE, (core + 1) * HEAD_SIZE)
            far = slice((1 - core) * HEAD_SIZE, (2 - core) * HEAD_SIZE)
            for i, (half_ref, out_ref) in enumerate(((near_dk_ref, dk_ref), (near_dv_ref, dv_ref))):
                out_ref[:, near] = half_ref[:, near]
                out_ref[:, far] = (swapped_ref[2 + i].astype(f32) + back_ref[i].astype(f32)).astype(bf16)


def join(kernel, name, shapes, steps, *operands):
    return pl.pallas_call(
        kernel,
        in_specs=[smem_spec()] + [vmem_spec()] * (len(operands) - 1),
        out_specs=[vmem_spec()] * len(shapes),
        out_shape=shapes,
        compiler_params=pltpu.CompilerParams(vmem_limit_bytes=16 << 20),
        cost_estimate=pl.CostEstimate(flops=steps << 20, transcendentals=0, bytes_accessed=1 << 20),
        name=name,
    )(*operands)


def first_allowed(doc_ids, chip):
    padded = jnp.concatenate([jnp.full((LOOKBACK_SPAN,), -1, jnp.int32), doc_ids])
    window = lax.dynamic_slice_in_dim(padded, chip * LOOKBACK_SPAN, 2 * LOOKBACK_SPAN, 0)
    own = window[LOOKBACK_SPAN:]
    document_start = jnp.sum((window[:, None] < own[None, :]).astype(jnp.int32), axis=0)
    reach_start = jnp.arange(1, LOOKBACK_SPAN + 1, dtype=jnp.int32)
    return jnp.maximum(document_start, reach_start).reshape(LOOKBACK_SPAN // CHUNK, 1, CHUNK)


def exchange(value):
    value = value.reshape((-1,) + value.shape[2:])
    return lax.all_to_all(value, ("core", "head"), split_axis=0, concat_axis=0, tiled=True)


def on_device(queries, keys, values, rows, grads, lse, doc_ids):
    chips = lax.axis_size("chip")
    groups = lax.axis_size("head")
    chip = lax.axis_index("chip")
    core = lax.axis_index("core").astype(jnp.int32).reshape(1)
    lo = first_allowed(doc_ids, chip)
    kv = exchange(pack_keys(keys, values, groups))
    packed = pack_queries(queries, grads, rows, lse, groups)
    kv, packed = lax.optimization_barrier((kv, packed))
    q = exchange(packed)
    kv_before = lax.ppermute(kv, "chip", [(c, c + 1) for c in range(chips - 1)])
    dq_part, near, far = cross_terms(core, kv_before, q, lo)
    back_near = lax.ppermute(near, "chip", [(c + 1, c) for c in range(chips - 1)])
    back_far = lax.ppermute(
        far,
        ("chip", "core"),
        [(CORES * (c + 1) + k, CORES * c + 1 - k) for c in range(chips - 1) for k in range(CORES)],
    )
    near_dq, own_near, own_far = own_terms(core, kv, q, lo, dq_part)
    swapped = lax.ppermute(own_far, "core", [(0, 1), (1, 0)])
    keys_shape = jax.ShapeDtypeStruct((HALF, 2 * HEAD_SIZE), bf16)
    queries_shape = jax.ShapeDtypeStruct((HALF, 4 * HEAD_SIZE), bf16)
    halves = join(join_near_kernel, "join_near", [keys_shape] * 2, 10000, core, own_near, back_near)
    return tuple(
        join(
            join_far_kernel, "join_far", [queries_shape, keys_shape, keys_shape], 1,
            core, near_dq, swapped, back_far, *halves,
        )
    )


def solution(mesh):
    seq, head = mesh.devices.shape
    fine = Mesh(mesh.devices.reshape(seq // CORES, CORES, head), ("chip", "core", "head"))
    tokens = ("chip", "core", "head")
    return jax.shard_map(
        on_device,
        mesh=fine,
        in_specs=(P(tokens), P(tokens), P(tokens), P(tokens), P(tokens), P(None, tokens), P()),
        out_specs=(P(("chip", "core"), "head"),) * 3,
        check_vma=False,
    )
```

```python
import math

import jax
import jax.numpy as jnp
from jax import lax
from jax.experimental import pallas as pl
from jax.experimental.pallas import tpu as pltpu
from jax.sharding import Mesh
from jax.sharding import PartitionSpec as P

HEAD_SIZE = 128
LOOKBACK_SPAN = 1024
CORES = 2
PIECE = 64
META_ROWS = 8
CHUNK = 128

score_scale = 168.0 ** (-0.5)
log2_e = math.log2(math.e)

f32 = jnp.float32
bf16 = jnp.bfloat16


def dot_t(left, right):
    return lax.dot_general(left, right, (((1,), (1,)), ((), ())), preferred_element_type=f32)


def dot_n(left, right):
    return lax.dot_general(left, right, (((1,), (0,)), ((), ())), preferred_element_type=f32)


def t_dot(left, right):
    return lax.dot_general(left, right, (((0,), (0,)), ((), ())), preferred_element_type=f32)


def pack_keys_kernel(key_ref, value_ref, out_ref):
    for at in range(CORES * out_ref.shape[1]):
        columns = slice(at * HEAD_SIZE, (at + 1) * HEAD_SIZE)
        out_ref[at % CORES, at // CORES, 0:PIECE, :] = key_ref[:, columns]
        out_ref[at % CORES, at // CORES, PIECE : 2 * PIECE, :] = value_ref[:, columns]


def pack_keys(keys, values, groups, steps=2):
    width = keys.shape[1] // steps
    return pl.pallas_call(
        pack_keys_kernel,
        grid=(steps,),
        in_specs=[pl.BlockSpec((PIECE, width), lambda i: (0, i))] * 2,
        out_specs=pl.BlockSpec((CORES, groups // steps, 2 * PIECE, HEAD_SIZE), lambda i: (0, i, 0, 0)),
        out_shape=jax.ShapeDtypeStruct((CORES, groups, 2 * PIECE, HEAD_SIZE), bf16),
        name="pack_keys",
    )(keys, values)


def three_parts(value):
    high = value.astype(bf16)
    rest = value - high.astype(f32)
    middle = rest.astype(bf16)
    return [high, middle, (rest - middle.astype(f32)).astype(bf16)]


def pack_queries_kernel(query_ref, grad_ref, row_ref, lse_ref, out_ref):
    groups = out_ref.shape[1]
    receivers = CORES * groups
    heads = 2 * receivers
    width = heads * HEAD_SIZE
    for at in range(receivers):
        for a in range(2):
            columns = slice((2 * at + a) * HEAD_SIZE, (2 * at + a + 1) * HEAD_SIZE)
            core, group = at % CORES, at // CORES
            out_ref[core, group, a * PIECE : (a + 1) * PIECE, :] = query_ref[:, columns]
            out_ref[core, group, (2 + a) * PIECE : (3 + a) * PIECE, :] = grad_ref[:, columns]
    product = grad_ref[...].astype(f32) * row_ref[...].astype(f32)
    product_high = product.astype(bf16)
    product_low = (product - product_high.astype(f32)).astype(bf16)
    which = lax.broadcasted_iota(jnp.int32, (heads, width), 1) // HEAD_SIZE
    member = jnp.where(which == lax.broadcasted_iota(jnp.int32, (heads, width), 0), 1.0, 0.0).astype(bf16)
    delta = dot_t(member, product_high) + dot_t(member, product_low)
    parts = three_parts(lse_ref[...]) + three_parts(delta)
    rows = jnp.concatenate([p.astype(f32) for p in parts], axis=0).astype(bf16)
    total = receivers * META_ROWS
    row_at = lax.broadcasted_iota(jnp.int32, (total, 6 * heads), 0)
    column_at = lax.broadcasted_iota(jnp.int32, (total, 6 * heads), 1)
    receiver = (row_at // META_ROWS) % groups * CORES + row_at // (META_ROWS * groups)
    halves = []
    for half in range(2):
        m = 2 * (row_at % META_ROWS) + half
        source = ((m // 6) * 3 + m % 3) * heads + 2 * receiver + (m // 3) % 2
        pick = jnp.where((m < 12) & (column_at == source), 1.0, 0.0).astype(bf16)
        halves.append(dot_n(pick, rows))
    meta = jnp.concatenate(halves, axis=1).reshape(CORES, groups, META_ROWS, HEAD_SIZE)
    for core in range(CORES):
        for group in range(groups):
            out_ref[core, group, 4 * PIECE : 4 * PIECE + META_ROWS, :] = meta[core, group].astype(bf16)


def pack_queries(queries, grads, rows, lse, groups, steps=4):
    width = queries.shape[1] // steps
    height = 4 * PIECE + META_ROWS
    return pl.pallas_call(
        pack_queries_kernel,
        grid=(steps,),
        in_specs=[pl.BlockSpec((PIECE, width), lambda i: (0, i))] * 3
        + [pl.BlockSpec((lse.shape[0] // steps, PIECE), lambda i: (i, 0))],
        out_specs=pl.BlockSpec((CORES, groups // steps, height, HEAD_SIZE), lambda i: (0, i, 0, 0)),
        out_shape=jax.ShapeDtypeStruct((CORES, groups, height, HEAD_SIZE), bf16),
        name="pack_queries",
    )(queries, grads, rows, lse)


def chunk_meta(ref, at):
    meta = [ref[2 * at + i, 4 * PIECE : 4 * PIECE + META_ROWS, :].astype(f32) for i in range(2)]
    turned = [pltpu.roll(m, PIECE, 1) for m in meta]
    left = lax.broadcasted_iota(jnp.int32, meta[0].shape, 1) < PIECE
    halves = (jnp.where(left, meta[0], turned[1]), jnp.where(left, turned[0], meta[1]))
    pieces = [halves[m % 2][m // 2 : m // 2 + 1] for m in range(12)]
    rows = [pieces[3 * r] + pieces[3 * r + 1] + pieces[3 * r + 2] for r in range(4)]
    return jnp.concatenate(rows[0:2], axis=1), jnp.concatenate(rows[2:4], axis=1)


def sweep(causal, key_base, kv_ref, q_ref, lo_ref, dk_ref, dv_ref, dq_ref, part_ref):
    pieces = CHUNK // PIECE
    chunks = LOOKBACK_SPAN // CHUNK
    order = range(chunks - 1, -1, -1) if causal else range(chunks)
    for n, at in enumerate(order):
        first, last = (0, at + 1) if causal else (at, chunks)
        strip = slice(first * CHUNK, last * CHUNK)
        height = (last - first) * CHUNK
        sources = slice(first * pieces, last * pieces)
        key = kv_ref[sources, 0:PIECE, :].reshape(height, HEAD_SIZE)
        value = kv_ref[sources, PIECE : 2 * PIECE, :].reshape(height, HEAD_SIZE)
        sources = slice(at * pieces, (at + 1) * pieces)

        def both(row):
            return jnp.concatenate(
                [q_ref[sources, (row + a) * PIECE : (row + a + 1) * PIECE, :].reshape(CHUNK, HEAD_SIZE) for a in range(2)]
            )

        query = both(0)
        grad = both(2)
        lse, delta = chunk_meta(q_ref, at)
        lse = lse * log2_e
        lo = lo_ref[at] - (key_base + first * CHUNK)
        lo = jnp.concatenate([lo, lo], axis=1)
        key_at = lax.broadcasted_iota(jnp.int32, (height, 2 * CHUNK), 0)
        allowed = key_at >= lo
        if causal:
            query_at = lax.broadcasted_iota(jnp.int32, (1, 2 * CHUNK), 1) % CHUNK + at * CHUNK
            allowed = allowed & (key_at <= query_at)
        scores = dot_t(key, query)
        prob = jnp.where(allowed, jnp.exp2(scores * (score_scale * log2_e) - lse), 0.0)
        prob_grad = dot_t(value, grad)
        score_grad = ((prob * score_scale) * (prob_grad - delta)).astype(bf16)
        dv = dot_n(prob.astype(bf16), grad)
        dk = dot_n(score_grad, query)
        if n == 0:
            dv_ref[strip, :] = dv
            dk_ref[strip, :] = dk
        else:
            dv_ref[strip, :] += dv
            dk_ref[strip, :] += dk
        dq = t_dot(score_grad, key)
        for a in range(2):
            mine = dq[a * CHUNK : (a + 1) * CHUNK]
            if part_ref is not None:
                mine = mine + part_ref[a, at * CHUNK : (at + 1) * CHUNK, :]
            dq_ref[a, at * CHUNK : (at + 1) * CHUNK, :] = mine


def cross_kernel(kv_ref, q_ref, lo_ref, dq_ref, back_ref, dk_ref, dv_ref):
    sweep(False, 0, kv_ref, q_ref, lo_ref, dk_ref, dv_ref, dq_ref, None)
    back_ref[0] = dk_ref[...].astype(bf16)
    back_ref[1] = dv_ref[...].astype(bf16)


def own_kernel(kv_ref, q_ref, lo_ref, part_ref, dq_ref, sums_ref, sum_ref):
    sweep(True, LOOKBACK_SPAN, kv_ref, q_ref, lo_ref, sums_ref.at[0], sums_ref.at[1], sum_ref, part_ref)
    dq_ref[...] = sum_ref[...].astype(bf16)


def finish_kernel(core_ref, dq_ref, sums_ref, back_ref, near_ref, far_ref):
    near = pl.ds(pl.multiple_of(core_ref[0] * HALF, HALF), HALF)
    far = pl.ds(pl.multiple_of((1 - core_ref[0]) * HALF, HALF), HALF)
    for i in range(2):
        near_ref[i] = dq_ref[i, near, :]
        far_ref[i] = dq_ref[i, far, :]
        for rows, out_ref in ((near, near_ref), (far, far_ref)):
            out_ref[2 + i] = (sums_ref[i, rows, :] + back_ref[i, rows, :].astype(f32)).astype(bf16)


def join_kernel(core_ref, near_ref, far_ref, dq_ref, dk_ref, dv_ref):
    for core in range(CORES):

        @pl.when(core_ref[0] == core)
        def _():
            for half_ref, k in ((near_ref, core), (far_ref, 1 - core)):
                for a in range(2):
                    at = 2 * k + a
                    dq_ref[:, at * HEAD_SIZE : (at + 1) * HEAD_SIZE] = half_ref[a]
                dk_ref[:, k * HEAD_SIZE : (k + 1) * HEAD_SIZE] = half_ref[2]
                dv_ref[:, k * HEAD_SIZE : (k + 1) * HEAD_SIZE] = half_ref[3]


def vmem_spec():
    return pl.BlockSpec(memory_space=pltpu.VMEM)


def smem_spec():
    return pl.BlockSpec(memory_space=pltpu.SMEM)


HALF = LOOKBACK_SPAN // CORES


def cost():
    pairs = LOOKBACK_SPAN * LOOKBACK_SPAN
    return pl.CostEstimate(flops=pairs * 5 * 2 * HEAD_SIZE, transcendentals=pairs, bytes_accessed=4 << 20)


def whole_call(kernel, name, shapes, operands, scratch=(), estimate=None, smem=0):
    return pl.pallas_call(
        kernel,
        in_specs=[smem_spec()] * smem + [vmem_spec()] * (len(operands) - smem),
        out_specs=[vmem_spec()] * len(shapes),
        out_shape=[jax.ShapeDtypeStruct(shape, kind) for shape, kind in shapes],
        scratch_shapes=scratch,
        compiler_params=pltpu.CompilerParams(vmem_limit_bytes=16 << 20),
        cost_estimate=estimate,
        name=name,
    )(*operands)


def cross_terms(kv, q, lo):
    shapes = [((2, LOOKBACK_SPAN, HEAD_SIZE), f32), ((2, LOOKBACK_SPAN, HEAD_SIZE), bf16)]
    scratch = [pltpu.VMEM((LOOKBACK_SPAN, HEAD_SIZE), f32)] * 2
    return whole_call(cross_kernel, "cross_terms", shapes, (kv, q, lo), scratch, cost())


def own_terms(kv, q, lo, part):
    shapes = [((2, LOOKBACK_SPAN, HEAD_SIZE), bf16), ((2, LOOKBACK_SPAN, HEAD_SIZE), f32)]
    scratch = [pltpu.VMEM((2, LOOKBACK_SPAN, HEAD_SIZE), f32)]
    return whole_call(own_kernel, "own_terms", shapes, (kv, q, lo, part), scratch, cost())


def finish(core, dq, sums, back):
    return whole_call(finish_kernel, "finish", [((4, HALF, HEAD_SIZE), bf16)] * 2, (core, dq, sums, back), smem=1)


def join(core, near, far):
    shapes = [((HALF, heads * HEAD_SIZE), bf16) for heads in (4, 2, 2)]
    return whole_call(join_kernel, "join", shapes, (core, near, far), smem=1)


def first_allowed(doc_ids, chip):
    padded = jnp.concatenate([jnp.full((LOOKBACK_SPAN,), -1, jnp.int32), doc_ids])
    window = lax.dynamic_slice_in_dim(padded, chip * LOOKBACK_SPAN, 2 * LOOKBACK_SPAN, 0)
    own = window[LOOKBACK_SPAN:]
    document_start = jnp.sum((window[:, None] < own[None, :]).astype(jnp.int32), axis=0)
    reach_start = jnp.arange(1, LOOKBACK_SPAN + 1, dtype=jnp.int32)
    return jnp.maximum(document_start, reach_start).reshape(LOOKBACK_SPAN // CHUNK, 1, CHUNK)


def exchange(value):
    value = value.reshape((-1,) + value.shape[2:])
    return lax.all_to_all(value, ("core", "head"), split_axis=0, concat_axis=0, tiled=True)


def on_device(queries, keys, values, rows, grads, lse, doc_ids):
    chips = lax.axis_size("chip")
    groups = lax.axis_size("head")
    chip = lax.axis_index("chip")
    core = lax.axis_index("core").astype(jnp.int32).reshape(1)
    lo = first_allowed(doc_ids, chip)
    kv = exchange(pack_keys(keys, values, groups))
    packed = pack_queries(queries, grads, rows, lse, groups)
    kv, packed = lax.optimization_barrier((kv, packed))
    q = exchange(packed)
    kv_before = lax.ppermute(kv, "chip", [(c, c + 1) for c in range(chips - 1)])
    dq_part, back = cross_terms(kv_before, q, lo)
    back = lax.ppermute(back, "chip", [(c + 1, c) for c in range(chips - 1)])
    dq, sums = own_terms(kv, q, lo, dq_part)
    near, far = finish(core, dq, sums, back)
    far = lax.ppermute(far, "core", [(0, 1), (1, 0)])
    return tuple(join(core, near, far))


def solution(mesh):
    seq, head = mesh.devices.shape
    fine = Mesh(mesh.devices.reshape(seq // CORES, CORES, head), ("chip", "core", "head"))
    tokens = ("chip", "core", "head")
    return jax.shard_map(
        on_device,
        mesh=fine,
        in_specs=(P(tokens), P(tokens), P(tokens), P(tokens), P(tokens), P(None, tokens), P()),
        out_specs=(P(("chip", "core"), "head"),) * 3,
        check_vma=False,
    )
```

```python
import functools
import math

import jax
import jax.numpy as jnp
from jax import lax
from jax.experimental import pallas as pl
from jax.experimental.pallas import tpu as pltpu
from jax.sharding import Mesh
from jax.sharding import PartitionSpec as P

HEAD_SIZE = 128
LOOKBACK_SPAN = 1024
CORES = 2
PIECE = 64
META_ROWS = 8
CHUNK = 128

score_scale = 168.0 ** (-0.5)
log2_e = math.log2(math.e)

f32 = jnp.float32
bf16 = jnp.bfloat16


def dot_t(left, right):
    return lax.dot_general(left, right, (((1,), (1,)), ((), ())), preferred_element_type=f32)


def dot_n(left, right):
    return lax.dot_general(left, right, (((1,), (0,)), ((), ())), preferred_element_type=f32)


def t_dot(left, right):
    return lax.dot_general(left, right, (((0,), (0,)), ((), ())), preferred_element_type=f32)


def pack_keys_kernel(key_ref, value_ref, out_ref):
    for at in range(CORES * out_ref.shape[1]):
        columns = slice(at * HEAD_SIZE, (at + 1) * HEAD_SIZE)
        out_ref[at % CORES, at // CORES, 0:PIECE, :] = key_ref[:, columns]
        out_ref[at % CORES, at // CORES, PIECE : 2 * PIECE, :] = value_ref[:, columns]


def pack_keys(keys, values, groups, steps=2):
    width = keys.shape[1] // steps
    return pl.pallas_call(
        pack_keys_kernel,
        grid=(steps,),
        in_specs=[pl.BlockSpec((PIECE, width), lambda i: (0, i))] * 2,
        out_specs=pl.BlockSpec((CORES, groups // steps, 2 * PIECE, HEAD_SIZE), lambda i: (0, i, 0, 0)),
        out_shape=jax.ShapeDtypeStruct((CORES, groups, 2 * PIECE, HEAD_SIZE), bf16),
        name="pack_keys",
    )(keys, values)


def three_parts(value):
    high = value.astype(bf16)
    rest = value - high.astype(f32)
    middle = rest.astype(bf16)
    return [high, middle, (rest - middle.astype(f32)).astype(bf16)]


def pack_queries_kernel(query_ref, grad_ref, row_ref, lse_ref, out_ref):
    groups = out_ref.shape[1]
    receivers = CORES * groups
    heads = 2 * receivers
    width = heads * HEAD_SIZE
    for at in range(receivers):
        for a in range(2):
            columns = slice((2 * at + a) * HEAD_SIZE, (2 * at + a + 1) * HEAD_SIZE)
            core, group = at % CORES, at // CORES
            out_ref[core, group, a * PIECE : (a + 1) * PIECE, :] = query_ref[:, columns]
            out_ref[core, group, (2 + a) * PIECE : (3 + a) * PIECE, :] = grad_ref[:, columns]
    product = grad_ref[...].astype(f32) * row_ref[...].astype(f32)
    product_high = product.astype(bf16)
    product_low = (product - product_high.astype(f32)).astype(bf16)
    which = lax.broadcasted_iota(jnp.int32, (heads, width), 1) // HEAD_SIZE
    member = jnp.where(which == lax.broadcasted_iota(jnp.int32, (heads, width), 0), 1.0, 0.0).astype(bf16)
    delta = dot_t(member, product_high) + dot_t(member, product_low)
    parts = three_parts(lse_ref[...]) + three_parts(delta)
    rows = jnp.concatenate([p.astype(f32) for p in parts], axis=0).astype(bf16)
    total = receivers * META_ROWS
    row_at = lax.broadcasted_iota(jnp.int32, (total, 6 * heads), 0)
    column_at = lax.broadcasted_iota(jnp.int32, (total, 6 * heads), 1)
    receiver = (row_at // META_ROWS) % groups * CORES + row_at // (META_ROWS * groups)
    halves = []
    for half in range(2):
        m = 2 * (row_at % META_ROWS) + half
        source = ((m // 6) * 3 + m % 3) * heads + 2 * receiver + (m // 3) % 2
        pick = jnp.where((m < 12) & (column_at == source), 1.0, 0.0).astype(bf16)
        halves.append(dot_n(pick, rows))
    meta = jnp.concatenate(halves, axis=1).reshape(CORES, groups, META_ROWS, HEAD_SIZE)
    for core in range(CORES):
        for group in range(groups):
            out_ref[core, group, 4 * PIECE : 4 * PIECE + META_ROWS, :] = meta[core, group].astype(bf16)


def pack_queries(queries, grads, rows, lse, groups, steps=4):
    width = queries.shape[1] // steps
    height = 4 * PIECE + META_ROWS
    return pl.pallas_call(
        pack_queries_kernel,
        grid=(steps,),
        in_specs=[pl.BlockSpec((PIECE, width), lambda i: (0, i))] * 3
        + [pl.BlockSpec((lse.shape[0] // steps, PIECE), lambda i: (i, 0))],
        out_specs=pl.BlockSpec((CORES, groups // steps, height, HEAD_SIZE), lambda i: (0, i, 0, 0)),
        out_shape=jax.ShapeDtypeStruct((CORES, groups, height, HEAD_SIZE), bf16),
        name="pack_queries",
    )(queries, grads, rows, lse)


def chunk_meta(ref, at):
    meta = [ref[2 * at + i, 4 * PIECE : 4 * PIECE + META_ROWS, :].astype(f32) for i in range(2)]
    turned = [pltpu.roll(m, PIECE, 1) for m in meta]
    left = lax.broadcasted_iota(jnp.int32, meta[0].shape, 1) < PIECE
    halves = (jnp.where(left, meta[0], turned[1]), jnp.where(left, turned[0], meta[1]))
    pieces = [halves[m % 2][m // 2 : m // 2 + 1] for m in range(12)]
    rows = [pieces[3 * r] + pieces[3 * r + 1] + pieces[3 * r + 2] for r in range(4)]
    return jnp.concatenate(rows[0:2], axis=1), jnp.concatenate(rows[2:4], axis=1)


def sweep(strips, causal, key_base, kv_ref, q_ref, lo_ref, dk_ref, dv_ref, dq_ref, part_ref):
    pieces = CHUNK // PIECE
    base = strips[0][1]
    for n, (at, first, last) in enumerate(strips):
        strip = slice((first - base) * CHUNK, (last - base) * CHUNK)
        height = (last - first) * CHUNK
        sources = slice(first * pieces, last * pieces)
        key = kv_ref[sources, 0:PIECE, :].reshape(height, HEAD_SIZE)
        value = kv_ref[sources, PIECE : 2 * PIECE, :].reshape(height, HEAD_SIZE)
        sources = slice(at * pieces, (at + 1) * pieces)

        def both(row):
            return jnp.concatenate(
                [q_ref[sources, (row + a) * PIECE : (row + a + 1) * PIECE, :].reshape(CHUNK, HEAD_SIZE) for a in range(2)]
            )

        query = both(0)
        grad = both(2)
        lse, delta = chunk_meta(q_ref, at)
        lse = lse * log2_e
        lo = lo_ref[at] - (key_base + first * CHUNK)
        lo = jnp.concatenate([lo, lo], axis=1)
        key_at = lax.broadcasted_iota(jnp.int32, (height, 2 * CHUNK), 0)
        allowed = key_at >= lo
        if causal:
            query_at = lax.broadcasted_iota(jnp.int32, (1, 2 * CHUNK), 1) % CHUNK + at * CHUNK
            allowed = allowed & (key_at <= query_at)
        scores = dot_t(key, query)
        prob = jnp.where(allowed, jnp.exp2(scores * (score_scale * log2_e) - lse), 0.0)
        prob_grad = dot_t(value, grad)
        score_grad = ((prob * score_scale) * (prob_grad - delta)).astype(bf16)
        dv = dot_n(prob.astype(bf16), grad)
        dk = dot_n(score_grad, query)
        if n == 0:
            dv_ref[strip, :] = dv
            dk_ref[strip, :] = dk
        else:
            dv_ref[strip, :] += dv
            dk_ref[strip, :] += dk
        dq = t_dot(score_grad, key)
        for a in range(2):
            mine = dq[a * CHUNK : (a + 1) * CHUNK]
            if part_ref is not None:
                mine = mine + part_ref[a, at * CHUNK : (at + 1) * CHUNK, :]
            dq_ref[a, at * CHUNK : (at + 1) * CHUNK, :] = mine


def cross_kernel(near, core_ref, kv_ref, q_ref, lo_ref, *refs):
    part_ref = None if near else refs[0]
    dq_ref, out_ref, dk_ref, dv_ref = refs[-4:]
    chunks = LOOKBACK_SPAN // CHUNK
    for block in range(CORES):

        @pl.when(core_ref[0] == (block if near else 1 - block))
        def _():
            start, end = block * chunks // CORES, (block + 1) * chunks // CORES
            sweep(
                [(at, max(at, start), end) for at in range(end)],
                False, 0, kv_ref, q_ref, lo_ref, dk_ref, dv_ref, dq_ref, part_ref,
            )
            rest = slice(end * CHUNK, LOOKBACK_SPAN)
            if end < chunks:
                dq_ref[:, rest, :] = jnp.zeros_like(dq_ref[:, rest, :]) if near else part_ref[:, rest, :]
            out_ref[0] = dk_ref[...].astype(bf16)
            out_ref[1] = dv_ref[...].astype(bf16)


def own_kernel(core_ref, kv_ref, q_ref, lo_ref, part_ref, near_dq_ref, near_ref, far_ref, dk_ref, dv_ref, dq_ref):
    chunks = LOOKBACK_SPAN // CHUNK
    sweep(
        [(at, 0, at + 1) for at in range(chunks - 1, -1, -1)],
        True, LOOKBACK_SPAN, kv_ref, q_ref, lo_ref, dk_ref, dv_ref, dq_ref, part_ref,
    )
    near = pl.ds(pl.multiple_of(core_ref[0] * HALF, HALF), HALF)
    far = pl.ds(pl.multiple_of((1 - core_ref[0]) * HALF, HALF), HALF)
    for a in range(2):
        near_dq_ref[a] = dq_ref[a, near, :].astype(bf16)
        far_ref[a] = dq_ref[a, far, :].astype(bf16)
    near_ref[0] = dk_ref[near, :]
    near_ref[1] = dv_ref[near, :]
    far_ref[2] = dk_ref[far, :].astype(bf16)
    far_ref[3] = dv_ref[far, :].astype(bf16)


def vmem_spec():
    return pl.BlockSpec(memory_space=pltpu.VMEM)


def smem_spec():
    return pl.BlockSpec(memory_space=pltpu.SMEM)


HALF = LOOKBACK_SPAN // CORES


def rows_scratch(rows):
    return [pltpu.VMEM((rows, HEAD_SIZE), f32)] * 2


def cost():
    pairs = LOOKBACK_SPAN * LOOKBACK_SPAN
    return pl.CostEstimate(flops=pairs * 5 * 2 * HEAD_SIZE, transcendentals=pairs, bytes_accessed=4 << 20)


def cross_terms(near, core, kv, q, lo, *part):
    return pl.pallas_call(
        functools.partial(cross_kernel, near),
        in_specs=[smem_spec()] + [vmem_spec()] * (3 + len(part)),
        out_specs=[vmem_spec()] * 2,
        out_shape=[
            jax.ShapeDtypeStruct((2, LOOKBACK_SPAN, HEAD_SIZE), f32),
            jax.ShapeDtypeStruct((2, HALF, HEAD_SIZE), bf16),
        ],
        scratch_shapes=rows_scratch(HALF),
        compiler_params=pltpu.CompilerParams(vmem_limit_bytes=20 << 20),
        cost_estimate=cost(),
        name="cross_near" if near else "cross_far",
    )(core, kv, q, lo, *part)


def own_terms(core, kv, q, lo, part):
    return pl.pallas_call(
        own_kernel,
        in_specs=[smem_spec()] + [vmem_spec()] * 4,
        out_specs=[vmem_spec()] * 3,
        out_shape=[
            jax.ShapeDtypeStruct((2, HALF, HEAD_SIZE), bf16),
            jax.ShapeDtypeStruct((2, HALF, HEAD_SIZE), f32),
            jax.ShapeDtypeStruct((4, HALF, HEAD_SIZE), bf16),
        ],
        scratch_shapes=rows_scratch(LOOKBACK_SPAN) + [pltpu.VMEM((2, LOOKBACK_SPAN, HEAD_SIZE), f32)],
        compiler_params=pltpu.CompilerParams(vmem_limit_bytes=20 << 20),
        cost_estimate=cost(),
        name="own_terms",
    )(core, kv, q, lo, part)


def join_near_kernel(core_ref, near_ref, back_ref, dk_ref, dv_ref):
    for core in range(CORES):

        @pl.when(core_ref[0] == core)
        def _():
            columns = slice(core * HEAD_SIZE, (core + 1) * HEAD_SIZE)
            for i, out_ref in enumerate((dk_ref, dv_ref)):
                out_ref[:, columns] = (near_ref[i] + back_ref[i].astype(f32)).astype(bf16)


def join_far_kernel(core_ref, near_dq_ref, swapped_ref, back_ref, near_dk_ref, near_dv_ref, dq_ref, dk_ref, dv_ref):
    for core in range(CORES):

        @pl.when(core_ref[0] == core)
        def _():
            for a in range(2):
                at = 2 * core + a
                dq_ref[:, at * HEAD_SIZE : (at + 1) * HEAD_SIZE] = near_dq_ref[a]
                at = 2 * (1 - core) + a
                dq_ref[:, at * HEAD_SIZE : (at + 1) * HEAD_SIZE] = swapped_ref[a]
            near = slice(core * HEAD_SIZE, (core + 1) * HEAD_SIZE)
            far = slice((1 - core) * HEAD_SIZE, (2 - core) * HEAD_SIZE)
            for i, (half_ref, out_ref) in enumerate(((near_dk_ref, dk_ref), (near_dv_ref, dv_ref))):
                out_ref[:, near] = half_ref[:, near]
                out_ref[:, far] = (swapped_ref[2 + i].astype(f32) + back_ref[i].astype(f32)).astype(bf16)


def join(kernel, name, shapes, steps, *operands):
    return pl.pallas_call(
        kernel,
        in_specs=[smem_spec()] + [vmem_spec()] * (len(operands) - 1),
        out_specs=[vmem_spec()] * len(shapes),
        out_shape=shapes,
        compiler_params=pltpu.CompilerParams(vmem_limit_bytes=16 << 20),
        cost_estimate=pl.CostEstimate(flops=steps << 20, transcendentals=0, bytes_accessed=1 << 20),
        name=name,
    )(*operands)


def first_allowed(doc_ids, chip):
    padded = jnp.concatenate([jnp.full((LOOKBACK_SPAN,), -1, jnp.int32), doc_ids])
    window = lax.dynamic_slice_in_dim(padded, chip * LOOKBACK_SPAN, 2 * LOOKBACK_SPAN, 0)
    own = window[LOOKBACK_SPAN:]
    document_start = jnp.sum((window[:, None] < own[None, :]).astype(jnp.int32), axis=0)
    reach_start = jnp.arange(1, LOOKBACK_SPAN + 1, dtype=jnp.int32)
    return jnp.maximum(document_start, reach_start).reshape(LOOKBACK_SPAN // CHUNK, 1, CHUNK)


def exchange(value):
    value = value.reshape((-1,) + value.shape[2:])
    return lax.all_to_all(value, ("core", "head"), split_axis=0, concat_axis=0, tiled=True)


def on_device(queries, keys, values, rows, grads, lse, doc_ids):
    chips = lax.axis_size("chip")
    groups = lax.axis_size("head")
    chip = lax.axis_index("chip")
    core = lax.axis_index("core").astype(jnp.int32).reshape(1)
    lo = first_allowed(doc_ids, chip)
    kv = exchange(pack_keys(keys, values, groups))
    packed = pack_queries(queries, grads, rows, lse, groups)
    kv, packed = lax.optimization_barrier((kv, packed))
    q = exchange(packed)
    kv_before = lax.ppermute(kv, "chip", [(c, c + 1) for c in range(chips - 1)])
    dq_part, near = cross_terms(True, core, kv_before, q, lo)
    back_near = lax.ppermute(near, "chip", [(c + 1, c) for c in range(chips - 1)])
    dq_part, far = cross_terms(False, core, kv_before, q, lo, dq_part)
    back_far = lax.ppermute(
        far,
        ("chip", "core"),
        [(CORES * (c + 1) + k, CORES * c + 1 - k) for c in range(chips - 1) for k in range(CORES)],
    )
    near_dq, own_near, own_far = own_terms(core, kv, q, lo, dq_part)
    swapped = lax.ppermute(own_far, "core", [(0, 1), (1, 0)])
    keys_shape = jax.ShapeDtypeStruct((HALF, 2 * HEAD_SIZE), bf16)
    queries_shape = jax.ShapeDtypeStruct((HALF, 4 * HEAD_SIZE), bf16)
    halves = join(join_near_kernel, "join_near", [keys_shape] * 2, 10000, core, own_near, back_near)
    return tuple(
        join(
            join_far_kernel, "join_far", [queries_shape, keys_shape, keys_shape], 1,
            core, near_dq, swapped, back_far, *halves,
        )
    )


def solution(mesh):
    seq, head = mesh.devices.shape
    fine = Mesh(mesh.devices.reshape(seq // CORES, CORES, head), ("chip", "core", "head"))
    tokens = ("chip", "core", "head")
    return jax.shard_map(
        on_device,
        mesh=fine,
        in_specs=(P(tokens), P(tokens), P(tokens), P(tokens), P(tokens), P(None, tokens), P()),
        out_specs=(P(("chip", "core"), "head"),) * 3,
        check_vma=False,
    )
```

```python
import functools
import math

import jax
import jax.numpy as jnp
from jax import lax
from jax.experimental import pallas as pl
from jax.experimental.pallas import tpu as pltpu
from jax.sharding import Mesh
from jax.sharding import PartitionSpec as P

HEAD_SIZE = 128
LOOKBACK_SPAN = 1024
CORES = 2
PIECE = 64
META_ROWS = 8
CHUNK = 128

score_scale = 168.0 ** (-0.5)
log2_e = math.log2(math.e)

f32 = jnp.float32
bf16 = jnp.bfloat16


def dot_t(left, right):
    return lax.dot_general(left, right, (((1,), (1,)), ((), ())), preferred_element_type=f32)


def dot_n(left, right):
    return lax.dot_general(left, right, (((1,), (0,)), ((), ())), preferred_element_type=f32)


def t_dot(left, right):
    return lax.dot_general(left, right, (((0,), (0,)), ((), ())), preferred_element_type=f32)


def pack_keys_kernel(key_ref, value_ref, out_ref):
    for at in range(CORES * out_ref.shape[1]):
        columns = slice(at * HEAD_SIZE, (at + 1) * HEAD_SIZE)
        out_ref[at % CORES, at // CORES, 0:PIECE, :] = key_ref[:, columns]
        out_ref[at % CORES, at // CORES, PIECE : 2 * PIECE, :] = value_ref[:, columns]


def pack_keys(keys, values, groups, steps=2):
    width = keys.shape[1] // steps
    return pl.pallas_call(
        pack_keys_kernel,
        grid=(steps,),
        in_specs=[pl.BlockSpec((PIECE, width), lambda i: (0, i))] * 2,
        out_specs=pl.BlockSpec((CORES, groups // steps, 2 * PIECE, HEAD_SIZE), lambda i: (0, i, 0, 0)),
        out_shape=jax.ShapeDtypeStruct((CORES, groups, 2 * PIECE, HEAD_SIZE), bf16),
        name="pack_keys",
    )(keys, values)


def three_parts(value):
    high = value.astype(bf16)
    rest = value - high.astype(f32)
    middle = rest.astype(bf16)
    return [high, middle, (rest - middle.astype(f32)).astype(bf16)]


def pack_queries_kernel(query_ref, grad_ref, row_ref, lse_ref, out_ref):
    groups = out_ref.shape[1]
    receivers = CORES * groups
    heads = 2 * receivers
    width = heads * HEAD_SIZE
    for at in range(receivers):
        for a in range(2):
            columns = slice((2 * at + a) * HEAD_SIZE, (2 * at + a + 1) * HEAD_SIZE)
            core, group = at % CORES, at // CORES
            out_ref[core, group, a * PIECE : (a + 1) * PIECE, :] = query_ref[:, columns]
            out_ref[core, group, (2 + a) * PIECE : (3 + a) * PIECE, :] = grad_ref[:, columns]
    product = grad_ref[...].astype(f32) * row_ref[...].astype(f32)
    product_high = product.astype(bf16)
    product_low = (product - product_high.astype(f32)).astype(bf16)
    which = lax.broadcasted_iota(jnp.int32, (heads, width), 1) // HEAD_SIZE
    member = jnp.where(which == lax.broadcasted_iota(jnp.int32, (heads, width), 0), 1.0, 0.0).astype(bf16)
    delta = dot_t(member, product_high) + dot_t(member, product_low)
    parts = three_parts(lse_ref[...]) + three_parts(delta)
    rows = jnp.concatenate([p.astype(f32) for p in parts], axis=0).astype(bf16)
    total = receivers * META_ROWS
    row_at = lax.broadcasted_iota(jnp.int32, (total, 6 * heads), 0)
    column_at = lax.broadcasted_iota(jnp.int32, (total, 6 * heads), 1)
    receiver = (row_at // META_ROWS) % groups * CORES + row_at // (META_ROWS * groups)
    halves = []
    for half in range(2):
        m = 2 * (row_at % META_ROWS) + half
        source = ((m // 6) * 3 + m % 3) * heads + 2 * receiver + (m // 3) % 2
        pick = jnp.where((m < 12) & (column_at == source), 1.0, 0.0).astype(bf16)
        halves.append(dot_n(pick, rows))
    meta = jnp.concatenate(halves, axis=1).reshape(CORES, groups, META_ROWS, HEAD_SIZE)
    for core in range(CORES):
        for group in range(groups):
            out_ref[core, group, 4 * PIECE : 4 * PIECE + META_ROWS, :] = meta[core, group].astype(bf16)


def pack_queries(queries, grads, rows, lse, groups, steps=4):
    width = queries.shape[1] // steps
    height = 4 * PIECE + META_ROWS
    return pl.pallas_call(
        pack_queries_kernel,
        grid=(steps,),
        in_specs=[pl.BlockSpec((PIECE, width), lambda i: (0, i))] * 3
        + [pl.BlockSpec((lse.shape[0] // steps, PIECE), lambda i: (i, 0))],
        out_specs=pl.BlockSpec((CORES, groups // steps, height, HEAD_SIZE), lambda i: (0, i, 0, 0)),
        out_shape=jax.ShapeDtypeStruct((CORES, groups, height, HEAD_SIZE), bf16),
        name="pack_queries",
    )(queries, grads, rows, lse)


def chunk_meta(ref, at):
    meta = [ref[2 * at + i, 4 * PIECE : 4 * PIECE + META_ROWS, :].astype(f32) for i in range(2)]
    turned = [pltpu.roll(m, PIECE, 1) for m in meta]
    left = lax.broadcasted_iota(jnp.int32, meta[0].shape, 1) < PIECE
    halves = (jnp.where(left, meta[0], turned[1]), jnp.where(left, turned[0], meta[1]))
    pieces = [halves[m % 2][m // 2 : m // 2 + 1] for m in range(12)]
    rows = [pieces[3 * r] + pieces[3 * r + 1] + pieces[3 * r + 2] for r in range(4)]
    return jnp.concatenate(rows[0:2], axis=1), jnp.concatenate(rows[2:4], axis=1)


def sweep(strips, causal, key_base, kv_ref, q_ref, lo_ref, dk_ref, dv_ref, dq_ref, part_ref, first_query=0):
    pieces = CHUNK // PIECE
    base = strips[0][1]
    for n, (at, first, last) in enumerate(strips):
        strip = slice((first - base) * CHUNK, (last - base) * CHUNK)
        height = (last - first) * CHUNK
        sources = slice(first * pieces, last * pieces)
        key = kv_ref[sources, 0:PIECE, :].reshape(height, HEAD_SIZE)
        value = kv_ref[sources, PIECE : 2 * PIECE, :].reshape(height, HEAD_SIZE)
        sources = slice(at * pieces, (at + 1) * pieces)

        def both(row):
            return jnp.concatenate(
                [q_ref[sources, (row + a) * PIECE : (row + a + 1) * PIECE, :].reshape(CHUNK, HEAD_SIZE) for a in range(2)]
            )

        query = both(0)
        grad = both(2)
        lse, delta = chunk_meta(q_ref, at)
        lse = lse * log2_e
        lo = lo_ref[at] - (key_base + first * CHUNK)
        lo = jnp.concatenate([lo, lo], axis=1)
        key_at = lax.broadcasted_iota(jnp.int32, (height, 2 * CHUNK), 0)
        allowed = key_at >= lo
        if causal:
            query_at = lax.broadcasted_iota(jnp.int32, (1, 2 * CHUNK), 1) % CHUNK + (at - first) * CHUNK
            allowed = allowed & (key_at <= query_at)
        scores = dot_t(key, query)
        prob = jnp.where(allowed, jnp.exp2(scores * (score_scale * log2_e) - lse), 0.0)
        prob_grad = dot_t(value, grad)
        score_grad = ((prob * score_scale) * (prob_grad - delta)).astype(bf16)
        dv = dot_n(prob.astype(bf16), grad)
        dk = dot_n(score_grad, query)
        if n == 0:
            dv_ref[strip, :] = dv
            dk_ref[strip, :] = dk
        else:
            dv_ref[strip, :] += dv
            dk_ref[strip, :] += dk
        dq = t_dot(score_grad, key)
        for a in range(2):
            mine = dq[a * CHUNK : (a + 1) * CHUNK]
            rows = slice((at - first_query) * CHUNK, (at - first_query + 1) * CHUNK)
            if part_ref is not None:
                mine = mine + part_ref[a, rows, :]
            dq_ref[a, rows, :] = mine


def cross_kernel(near, core_ref, kv_ref, q_ref, lo_ref, *refs):
    part_ref = None if near else refs[0]
    dq_ref, out_ref, dk_ref, dv_ref = refs[-4:]
    chunks = LOOKBACK_SPAN // CHUNK
    for block in range(CORES):

        @pl.when(core_ref[0] == (block if near else 1 - block))
        def _():
            start, end = block * chunks // CORES, (block + 1) * chunks // CORES
            sweep(
                [(at, max(at, start), end) for at in range(end)],
                False, 0, kv_ref, q_ref, lo_ref, dk_ref, dv_ref, dq_ref, part_ref,
            )
            rest = slice(end * CHUNK, LOOKBACK_SPAN)
            if end < chunks:
                dq_ref[:, rest, :] = jnp.zeros_like(dq_ref[:, rest, :]) if near else part_ref[:, rest, :]
            out_ref[0] = dk_ref[...].astype(bf16)
            out_ref[1] = dv_ref[...].astype(bf16)


def own_far_kernel(core_ref, kv_ref, q_ref, lo_ref, part_ref, far_ref, near_dq_ref, near_ref, dk_ref, dv_ref, dq_ref):
    chunks = LOOKBACK_SPAN // CHUNK
    half = chunks // CORES
    upper = [(at, 0, at + 1) for at in range(chunks - 1, half - 1, -1)]
    across = [(at, 0, half) for at in range(half, chunks)]
    lower = [(at, 0, at + 1) for at in range(half)]
    for core, strips in enumerate((upper, across + lower)):

        @pl.when(core_ref[0] == core)
        def _():
            sweep(
                strips, True, LOOKBACK_SPAN, kv_ref, q_ref, lo_ref, dk_ref, dv_ref, dq_ref, part_ref,
            )
            near = slice(core * HALF, (core + 1) * HALF)
            far = slice((1 - core) * HALF, (2 - core) * HALF)
            near_dq_ref[...] = part_ref[:, near, :] if core == 0 else dq_ref[:, near, :]
            far_ref[0:2] = dq_ref[:, far, :].astype(bf16)
            for i, sum_ref in enumerate((dk_ref, dv_ref)):
                far_ref[2 + i] = sum_ref[far, :].astype(bf16)
                near_ref[i] = sum_ref[near, :] if core == 0 else jnp.zeros_like(near_ref[i])


def own_near_kernel(core_ref, kv_ref, q_ref, lo_ref, part_dq_ref, part_ref, dq_out_ref, near_ref, dk_ref, dv_ref, dq_ref):
    chunks = LOOKBACK_SPAN // CHUNK
    half = chunks // CORES
    for core in range(CORES):

        @pl.when(core_ref[0] == core)
        def _():
            start = core * half
            sweep(
                [(at, start, at + 1) for at in range(start + half - 1, start - 1, -1)],
                True, LOOKBACK_SPAN, kv_ref, q_ref, lo_ref, dk_ref, dv_ref, dq_ref, part_dq_ref, start,
            )

    dq_out_ref[...] = dq_ref[...].astype(bf16)
    near_ref[0] = part_ref[0] + dk_ref[...]
    near_ref[1] = part_ref[1] + dv_ref[...]


def vmem_spec():
    return pl.BlockSpec(memory_space=pltpu.VMEM)


def smem_spec():
    return pl.BlockSpec(memory_space=pltpu.SMEM)


HALF = LOOKBACK_SPAN // CORES


def rows_scratch(rows):
    return [pltpu.VMEM((rows, HEAD_SIZE), f32)] * 2


def cost():
    pairs = LOOKBACK_SPAN * LOOKBACK_SPAN
    return pl.CostEstimate(flops=pairs * 5 * 2 * HEAD_SIZE, transcendentals=pairs, bytes_accessed=4 << 20)


def cross_terms(near, core, kv, q, lo, *part):
    return pl.pallas_call(
        functools.partial(cross_kernel, near),
        in_specs=[smem_spec()] + [vmem_spec()] * (3 + len(part)),
        out_specs=[vmem_spec()] * 2,
        out_shape=[
            jax.ShapeDtypeStruct((2, LOOKBACK_SPAN, HEAD_SIZE), f32),
            jax.ShapeDtypeStruct((2, HALF, HEAD_SIZE), bf16),
        ],
        scratch_shapes=rows_scratch(HALF),
        compiler_params=pltpu.CompilerParams(vmem_limit_bytes=20 << 20),
        cost_estimate=cost(),
        name="cross_near" if near else "cross_far",
    )(core, kv, q, lo, *part)


def own_call(kernel, name, shapes, rows, *operands):
    return pl.pallas_call(
        kernel,
        in_specs=[smem_spec()] + [vmem_spec()] * (len(operands) - 1),
        out_specs=[vmem_spec()] * len(shapes),
        out_shape=[jax.ShapeDtypeStruct((count, HALF, HEAD_SIZE), kind) for count, kind in shapes],
        scratch_shapes=rows_scratch(rows) + [pltpu.VMEM((2, rows, HEAD_SIZE), f32)],
        compiler_params=pltpu.CompilerParams(vmem_limit_bytes=20 << 20),
        cost_estimate=cost(),
        name=name,
    )(*operands)


def join_near_kernel(core_ref, near_ref, back_ref, dk_ref, dv_ref):
    for core in range(CORES):

        @pl.when(core_ref[0] == core)
        def _():
            columns = slice(core * HEAD_SIZE, (core + 1) * HEAD_SIZE)
            for i, out_ref in enumerate((dk_ref, dv_ref)):
                out_ref[:, columns] = (near_ref[i] + back_ref[i].astype(f32)).astype(bf16)


def join_far_kernel(core_ref, near_dq_ref, swapped_ref, back_ref, near_dk_ref, near_dv_ref, dq_ref, dk_ref, dv_ref):
    for core in range(CORES):

        @pl.when(core_ref[0] == core)
        def _():
            for a in range(2):
                at = 2 * core + a
                dq_ref[:, at * HEAD_SIZE : (at + 1) * HEAD_SIZE] = near_dq_ref[a]
                at = 2 * (1 - core) + a
                dq_ref[:, at * HEAD_SIZE : (at + 1) * HEAD_SIZE] = swapped_ref[a]
            near = slice(core * HEAD_SIZE, (core + 1) * HEAD_SIZE)
            far = slice((1 - core) * HEAD_SIZE, (2 - core) * HEAD_SIZE)
            for i, (half_ref, out_ref) in enumerate(((near_dk_ref, dk_ref), (near_dv_ref, dv_ref))):
                out_ref[:, near] = half_ref[:, near]
                out_ref[:, far] = (swapped_ref[2 + i].astype(f32) + back_ref[i].astype(f32)).astype(bf16)


def join(kernel, name, shapes, steps, *operands):
    return pl.pallas_call(
        kernel,
        in_specs=[smem_spec()] + [vmem_spec()] * (len(operands) - 1),
        out_specs=[vmem_spec()] * len(shapes),
        out_shape=shapes,
        compiler_params=pltpu.CompilerParams(vmem_limit_bytes=16 << 20),
        cost_estimate=pl.CostEstimate(flops=steps << 20, transcendentals=0, bytes_accessed=1 << 20),
        name=name,
    )(*operands)


def first_allowed(doc_ids, chip):
    padded = jnp.concatenate([jnp.full((LOOKBACK_SPAN,), -1, jnp.int32), doc_ids])
    window = lax.dynamic_slice_in_dim(padded, chip * LOOKBACK_SPAN, 2 * LOOKBACK_SPAN, 0)
    own = window[LOOKBACK_SPAN:]
    document_start = jnp.sum((window[:, None] < own[None, :]).astype(jnp.int32), axis=0)
    reach_start = jnp.arange(1, LOOKBACK_SPAN + 1, dtype=jnp.int32)
    return jnp.maximum(document_start, reach_start).reshape(LOOKBACK_SPAN // CHUNK, 1, CHUNK)


def exchange(value):
    value = value.reshape((-1,) + value.shape[2:])
    return lax.all_to_all(value, ("core", "head"), split_axis=0, concat_axis=0, tiled=True)


def on_device(queries, keys, values, rows, grads, lse, doc_ids):
    chips = lax.axis_size("chip")
    groups = lax.axis_size("head")
    chip = lax.axis_index("chip")
    core = lax.axis_index("core").astype(jnp.int32).reshape(1)
    lo = first_allowed(doc_ids, chip)
    kv = exchange(pack_keys(keys, values, groups))
    packed = pack_queries(queries, grads, rows, lse, groups)
    kv, packed = lax.optimization_barrier((kv, packed))
    q = exchange(packed)
    kv_before = lax.ppermute(kv, "chip", [(c, c + 1) for c in range(chips - 1)])
    dq_part, near = cross_terms(True, core, kv_before, q, lo)
    back_near = lax.ppermute(near, "chip", [(c + 1, c) for c in range(chips - 1)])
    dq_part, far = cross_terms(False, core, kv_before, q, lo, dq_part)
    back_far = lax.ppermute(
        far,
        ("chip", "core"),
        [(CORES * (c + 1) + k, CORES * c + 1 - k) for c in range(chips - 1) for k in range(CORES)],
    )
    own_far, near_dq, own_near = own_call(
        own_far_kernel, "own_far", [(4, bf16), (2, f32), (2, f32)], LOOKBACK_SPAN, core, kv, q, lo, dq_part
    )
    swapped = lax.ppermute(own_far, "core", [(0, 1), (1, 0)])
    near_dq, own_near = own_call(
        own_near_kernel, "own_near", [(2, bf16), (2, f32)], HALF, core, kv, q, lo, near_dq, own_near
    )
    keys_shape = jax.ShapeDtypeStruct((HALF, 2 * HEAD_SIZE), bf16)
    queries_shape = jax.ShapeDtypeStruct((HALF, 4 * HEAD_SIZE), bf16)
    halves = join(join_near_kernel, "join_near", [keys_shape] * 2, 10000, core, own_near, back_near)
    return tuple(
        join(
            join_far_kernel, "join_far", [queries_shape, keys_shape, keys_shape], 1,
            core, near_dq, swapped, back_far, *halves,
        )
    )


def solution(mesh):
    seq, head = mesh.devices.shape
    fine = Mesh(mesh.devices.reshape(seq // CORES, CORES, head), ("chip", "core", "head"))
    tokens = ("chip", "core", "head")
    return jax.shard_map(
        on_device,
        mesh=fine,
        in_specs=(P(tokens), P(tokens), P(tokens), P(tokens), P(tokens), P(None, tokens), P()),
        out_specs=(P(("chip", "core"), "head"),) * 3,
        check_vma=False,
    )
```

```python
import functools
import math

import jax
import jax.numpy as jnp
from jax import lax
from jax.experimental import pallas as pl
from jax.experimental.pallas import tpu as pltpu
from jax.sharding import Mesh
from jax.sharding import PartitionSpec as P

HEAD_SIZE = 128
LOOKBACK_SPAN = 1024
CORES = 2
PIECE = 64
META_ROWS = 8
CHUNK = 128

score_scale = 168.0 ** (-0.5)
log2_e = math.log2(math.e)

f32 = jnp.float32
bf16 = jnp.bfloat16


def dot_t(left, right):
    return lax.dot_general(left, right, (((1,), (1,)), ((), ())), preferred_element_type=f32)


def dot_n(left, right):
    return lax.dot_general(left, right, (((1,), (0,)), ((), ())), preferred_element_type=f32)


def t_dot(left, right):
    return lax.dot_general(left, right, (((0,), (0,)), ((), ())), preferred_element_type=f32)


def pack_keys_kernel(key_ref, value_ref, out_ref):
    for at in range(out_ref.shape[0]):
        columns = slice(at * HEAD_SIZE, (at + 1) * HEAD_SIZE)
        out_ref[at, 0:PIECE, :] = key_ref[:, columns]
        out_ref[at, PIECE : 2 * PIECE, :] = value_ref[:, columns]


def pack_keys(keys, values, steps=2):
    heads = keys.shape[1] // HEAD_SIZE
    return pl.pallas_call(
        pack_keys_kernel,
        grid=(steps,),
        in_specs=[pl.BlockSpec((PIECE, keys.shape[1] // steps), lambda i: (0, i))] * 2,
        out_specs=pl.BlockSpec((heads // steps, 2 * PIECE, HEAD_SIZE), lambda i: (i, 0, 0)),
        out_shape=jax.ShapeDtypeStruct((heads, 2 * PIECE, HEAD_SIZE), bf16),
        name="pack_keys",
    )(keys, values)


def three_parts(value):
    high = value.astype(bf16)
    rest = value - high.astype(f32)
    middle = rest.astype(bf16)
    return [high, middle, (rest - middle.astype(f32)).astype(bf16)]


def pack_queries_kernel(query_ref, grad_ref, row_ref, lse_ref, out_ref):
    groups = out_ref.shape[1]
    receivers = CORES * groups
    heads = 2 * receivers
    width = heads * HEAD_SIZE
    for at in range(receivers):
        for a in range(2):
            columns = slice((2 * at + a) * HEAD_SIZE, (2 * at + a + 1) * HEAD_SIZE)
            core, group = at % CORES, at // CORES
            out_ref[core, group, a * PIECE : (a + 1) * PIECE, :] = query_ref[:, columns]
            out_ref[core, group, (2 + a) * PIECE : (3 + a) * PIECE, :] = grad_ref[:, columns]
    product = grad_ref[...].astype(f32) * row_ref[...].astype(f32)
    product_high = product.astype(bf16)
    product_low = (product - product_high.astype(f32)).astype(bf16)
    which = lax.broadcasted_iota(jnp.int32, (heads, width), 1) // HEAD_SIZE
    member = jnp.where(which == lax.broadcasted_iota(jnp.int32, (heads, width), 0), 1.0, 0.0).astype(bf16)
    delta = dot_t(member, product_high) + dot_t(member, product_low)
    parts = three_parts(lse_ref[...]) + three_parts(delta)
    rows = jnp.concatenate([p.astype(f32) for p in parts], axis=0).astype(bf16)
    total = receivers * META_ROWS
    row_at = lax.broadcasted_iota(jnp.int32, (total, 6 * heads), 0)
    column_at = lax.broadcasted_iota(jnp.int32, (total, 6 * heads), 1)
    receiver = (row_at // META_ROWS) % groups * CORES + row_at // (META_ROWS * groups)
    halves = []
    for half in range(2):
        m = 2 * (row_at % META_ROWS) + half
        source = ((m // 6) * 3 + m % 3) * heads + 2 * receiver + (m // 3) % 2
        pick = jnp.where((m < 12) & (column_at == source), 1.0, 0.0).astype(bf16)
        halves.append(dot_n(pick, rows))
    meta = jnp.concatenate(halves, axis=1).reshape(CORES, groups, META_ROWS, HEAD_SIZE)
    for core in range(CORES):
        for group in range(groups):
            out_ref[core, group, 4 * PIECE : 4 * PIECE + META_ROWS, :] = meta[core, group].astype(bf16)


def pack_queries(queries, grads, rows, lse, groups, steps=4):
    width = queries.shape[1] // steps
    height = 4 * PIECE + META_ROWS
    return pl.pallas_call(
        pack_queries_kernel,
        grid=(steps,),
        in_specs=[pl.BlockSpec((PIECE, width), lambda i: (0, i))] * 3
        + [pl.BlockSpec((lse.shape[0] // steps, PIECE), lambda i: (i, 0))],
        out_specs=pl.BlockSpec((CORES, groups // steps, height, HEAD_SIZE), lambda i: (0, i, 0, 0)),
        out_shape=jax.ShapeDtypeStruct((CORES, groups, height, HEAD_SIZE), bf16),
        name="pack_queries",
    )(queries, grads, rows, lse)


def chunk_meta(ref, at):
    meta = [ref[2 * at + i, 4 * PIECE : 4 * PIECE + META_ROWS, :].astype(f32) for i in range(2)]
    turned = [pltpu.roll(m, PIECE, 1) for m in meta]
    left = lax.broadcasted_iota(jnp.int32, meta[0].shape, 1) < PIECE
    halves = (jnp.where(left, meta[0], turned[1]), jnp.where(left, turned[0], meta[1]))
    pieces = [halves[m % 2][m // 2 : m // 2 + 1] for m in range(12)]
    rows = [pieces[3 * r] + pieces[3 * r + 1] + pieces[3 * r + 2] for r in range(4)]
    return jnp.concatenate(rows[0:2], axis=1), jnp.concatenate(rows[2:4], axis=1)


def key_rows(refs, first, last, row):
    per_block = LOOKBACK_SPAN // CORES // CHUNK
    pieces = CHUNK // PIECE
    found = []
    for block in range(CORES):
        start, end = max(first, block * per_block), min(last, (block + 1) * per_block)
        if start < end:
            at = slice((start - block * per_block) * pieces, (end - block * per_block) * pieces)
            found.append(refs[block][at, row : row + PIECE, :].reshape((end - start) * CHUNK, HEAD_SIZE))
    return found[0] if len(found) == 1 else jnp.concatenate(found)


def sweep(strips, causal, key_base, kv_refs, q_ref, lo_ref, dk_ref, dv_ref, dq_ref, part_ref, first_query=0):
    pieces = CHUNK // PIECE
    base = strips[0][1]
    for n, (at, first, last) in enumerate(strips):
        strip = slice((first - base) * CHUNK, (last - base) * CHUNK)
        height = (last - first) * CHUNK
        key = key_rows(kv_refs, first, last, 0)
        value = key_rows(kv_refs, first, last, PIECE)
        sources = slice(at * pieces, (at + 1) * pieces)

        def both(row):
            return jnp.concatenate(
                [q_ref[sources, (row + a) * PIECE : (row + a + 1) * PIECE, :].reshape(CHUNK, HEAD_SIZE) for a in range(2)]
            )

        query = both(0)
        grad = both(2)
        lse, delta = chunk_meta(q_ref, at)
        lse = lse * log2_e
        lo = lo_ref[at] - (key_base + first * CHUNK)
        lo = jnp.concatenate([lo, lo], axis=1)
        key_at = lax.broadcasted_iota(jnp.int32, (height, 2 * CHUNK), 0)
        allowed = key_at >= lo
        if causal:
            query_at = lax.broadcasted_iota(jnp.int32, (1, 2 * CHUNK), 1) % CHUNK + (at - first) * CHUNK
            allowed = allowed & (key_at <= query_at)
        scores = dot_t(key, query)
        prob = jnp.where(allowed, jnp.exp2(scores * (score_scale * log2_e) - lse), 0.0)
        prob_grad = dot_t(value, grad)
        score_grad = ((prob * score_scale) * (prob_grad - delta)).astype(bf16)
        dv = dot_n(prob.astype(bf16), grad)
        dk = dot_n(score_grad, query)
        if n == 0:
            dv_ref[strip, :] = dv
            dk_ref[strip, :] = dk
        else:
            dv_ref[strip, :] += dv
            dk_ref[strip, :] += dk
        dq = t_dot(score_grad, key)
        for a in range(2):
            mine = dq[a * CHUNK : (a + 1) * CHUNK]
            rows = slice((at - first_query) * CHUNK, (at - first_query + 1) * CHUNK)
            if part_ref is not None:
                mine = mine + part_ref[a, rows, :]
            dq_ref[a, rows, :] = mine


def cross_kernel(near, core_ref, kv_ref, q_ref, lo_ref, *refs):
    part_ref = None if near else refs[0]
    dq_ref, out_ref, dk_ref, dv_ref = refs[-4:]
    chunks = LOOKBACK_SPAN // CHUNK
    for block in range(CORES):

        @pl.when(core_ref[0] == (block if near else 1 - block))
        def _():
            start, end = block * chunks // CORES, (block + 1) * chunks // CORES
            sweep(
                [(at, max(at, start), end) for at in range(end)],
                False, 0, (kv_ref, kv_ref), q_ref, lo_ref, dk_ref, dv_ref, dq_ref, part_ref,
            )
            rest = slice(end * CHUNK, LOOKBACK_SPAN)
            if end < chunks:
                dq_ref[:, rest, :] = jnp.zeros_like(dq_ref[:, rest, :]) if near else part_ref[:, rest, :]
            out_ref[0] = dk_ref[...].astype(bf16)
            out_ref[1] = dv_ref[...].astype(bf16)


def own_far_kernel(core_ref, kv_near_ref, kv_far_ref, q_ref, lo_ref, part_ref, far_ref, near_dq_ref, near_ref, dk_ref, dv_ref, dq_ref):
    chunks = LOOKBACK_SPAN // CHUNK
    half = chunks // CORES
    upper = [(at, 0, at + 1) for at in range(chunks - 1, half - 1, -1)]
    across = [(at, 0, half) for at in range(half, chunks)]
    lower = [(at, 0, at + 1) for at in range(half)]
    for core, strips in enumerate((upper, across + lower)):

        @pl.when(core_ref[0] == core)
        def _():
            kv_refs = (kv_near_ref, kv_far_ref) if core == 0 else (kv_far_ref, kv_near_ref)
            sweep(
                strips, True, LOOKBACK_SPAN, kv_refs, q_ref, lo_ref, dk_ref, dv_ref, dq_ref, part_ref,
            )
            near = slice(core * HALF, (core + 1) * HALF)
            far = slice((1 - core) * HALF, (2 - core) * HALF)
            near_dq_ref[...] = part_ref[:, near, :] if core == 0 else dq_ref[:, near, :]
            far_ref[0:2] = dq_ref[:, far, :].astype(bf16)
            for i, sum_ref in enumerate((dk_ref, dv_ref)):
                far_ref[2 + i] = sum_ref[far, :].astype(bf16)
                near_ref[i] = sum_ref[near, :] if core == 0 else jnp.zeros_like(near_ref[i])


def own_near_kernel(core_ref, kv_ref, q_ref, lo_ref, part_dq_ref, part_ref, dq_out_ref, near_ref, dk_ref, dv_ref, dq_ref):
    chunks = LOOKBACK_SPAN // CHUNK
    half = chunks // CORES
    for core in range(CORES):

        @pl.when(core_ref[0] == core)
        def _():
            start = core * half
            sweep(
                [(at, start, at + 1) for at in range(start + half - 1, start - 1, -1)],
                True, LOOKBACK_SPAN, (kv_ref, kv_ref), q_ref, lo_ref, dk_ref, dv_ref, dq_ref, part_dq_ref, start,
            )

    dq_out_ref[...] = dq_ref[...].astype(bf16)
    near_ref[0] = part_ref[0] + dk_ref[...]
    near_ref[1] = part_ref[1] + dv_ref[...]


def vmem_spec():
    return pl.BlockSpec(memory_space=pltpu.VMEM)


def smem_spec():
    return pl.BlockSpec(memory_space=pltpu.SMEM)


HALF = LOOKBACK_SPAN // CORES


def rows_scratch(rows):
    return [pltpu.VMEM((rows, HEAD_SIZE), f32)] * 2


def cost():
    pairs = LOOKBACK_SPAN * LOOKBACK_SPAN
    return pl.CostEstimate(flops=pairs * 5 * 2 * HEAD_SIZE, transcendentals=pairs, bytes_accessed=4 << 20)


def cross_terms(near, core, kv, q, lo, *part):
    return pl.pallas_call(
        functools.partial(cross_kernel, near),
        in_specs=[smem_spec()] + [vmem_spec()] * (3 + len(part)),
        out_specs=[vmem_spec()] * 2,
        out_shape=[
            jax.ShapeDtypeStruct((2, LOOKBACK_SPAN, HEAD_SIZE), f32),
            jax.ShapeDtypeStruct((2, HALF, HEAD_SIZE), bf16),
        ],
        scratch_shapes=rows_scratch(HALF),
        compiler_params=pltpu.CompilerParams(vmem_limit_bytes=20 << 20),
        cost_estimate=cost(),
        name="cross_near" if near else "cross_far",
    )(core, kv, q, lo, *part)


def own_call(kernel, name, shapes, rows, *operands):
    return pl.pallas_call(
        kernel,
        in_specs=[smem_spec()] + [vmem_spec()] * (len(operands) - 1),
        out_specs=[vmem_spec()] * len(shapes),
        out_shape=[jax.ShapeDtypeStruct((count, HALF, HEAD_SIZE), kind) for count, kind in shapes],
        scratch_shapes=rows_scratch(rows) + [pltpu.VMEM((2, rows, HEAD_SIZE), f32)],
        compiler_params=pltpu.CompilerParams(vmem_limit_bytes=20 << 20),
        cost_estimate=cost(),
        name=name,
    )(*operands)


def join_near_kernel(core_ref, near_ref, back_ref, dk_ref, dv_ref):
    for core in range(CORES):

        @pl.when(core_ref[0] == core)
        def _():
            columns = slice(core * HEAD_SIZE, (core + 1) * HEAD_SIZE)
            for i, out_ref in enumerate((dk_ref, dv_ref)):
                out_ref[:, columns] = (near_ref[i] + back_ref[i].astype(f32)).astype(bf16)


def join_far_kernel(core_ref, near_dq_ref, swapped_ref, back_ref, near_dk_ref, near_dv_ref, dq_ref, dk_ref, dv_ref):
    for core in range(CORES):

        @pl.when(core_ref[0] == core)
        def _():
            for a in range(2):
                at = 2 * core + a
                dq_ref[:, at * HEAD_SIZE : (at + 1) * HEAD_SIZE] = near_dq_ref[a]
                at = 2 * (1 - core) + a
                dq_ref[:, at * HEAD_SIZE : (at + 1) * HEAD_SIZE] = swapped_ref[a]
            near = slice(core * HEAD_SIZE, (core + 1) * HEAD_SIZE)
            far = slice((1 - core) * HEAD_SIZE, (2 - core) * HEAD_SIZE)
            for i, (half_ref, out_ref) in enumerate(((near_dk_ref, dk_ref), (near_dv_ref, dv_ref))):
                out_ref[:, near] = half_ref[:, near]
                out_ref[:, far] = (swapped_ref[2 + i].astype(f32) + back_ref[i].astype(f32)).astype(bf16)


def join(kernel, name, shapes, steps, *operands):
    return pl.pallas_call(
        kernel,
        in_specs=[smem_spec()] + [vmem_spec()] * (len(operands) - 1),
        out_specs=[vmem_spec()] * len(shapes),
        out_shape=shapes,
        compiler_params=pltpu.CompilerParams(vmem_limit_bytes=16 << 20),
        cost_estimate=pl.CostEstimate(flops=steps << 20, transcendentals=0, bytes_accessed=1 << 20),
        name=name,
    )(*operands)


def first_allowed(doc_ids, chip):
    padded = jnp.concatenate([jnp.full((LOOKBACK_SPAN,), -1, jnp.int32), doc_ids])
    window = lax.dynamic_slice_in_dim(padded, chip * LOOKBACK_SPAN, 2 * LOOKBACK_SPAN, 0)
    own = window[LOOKBACK_SPAN:]
    document_start = jnp.sum((window[:, None] < own[None, :]).astype(jnp.int32), axis=0)
    reach_start = jnp.arange(1, LOOKBACK_SPAN + 1, dtype=jnp.int32)
    return jnp.maximum(document_start, reach_start).reshape(LOOKBACK_SPAN // CHUNK, 1, CHUNK)


def exchange(value, axes):
    return lax.all_to_all(value, axes, split_axis=0, concat_axis=0, tiled=True)


def other_core(value):
    return lax.ppermute(value, "core", [(0, 1), (1, 0)])


def next_chip(value, step, cross):
    chips = lax.axis_size("chip")
    pairs = [
        (CORES * c + k, CORES * (c + step) + (1 - k if cross else k))
        for c in range(max(0, -step), min(chips, chips - step))
        for k in range(CORES)
    ]
    return lax.ppermute(value, ("chip", "core"), pairs)


def on_device(queries, keys, values, rows, grads, lse, doc_ids):
    groups = lax.axis_size("head")
    chip = lax.axis_index("chip")
    core_at = lax.axis_index("core").astype(jnp.int32)
    core = core_at.reshape(1)
    lo = first_allowed(doc_ids, chip)
    kv = exchange(pack_keys(keys, values).reshape(groups, CORES, 2 * PIECE, HEAD_SIZE), "head")
    packed = pack_queries(queries, grads, rows, lse, groups)
    packed = packed.reshape((-1,) + packed.shape[2:])
    kv, packed = lax.optimization_barrier((kv, packed))
    q = exchange(packed, ("core", "head"))
    kv_near = jnp.where(core_at == 0, kv[:, 0], kv[:, 1])
    kv_give = jnp.where(core_at == 0, kv[:, 1], kv[:, 0])
    before_near = next_chip(kv_near, 1, False)
    before_far = next_chip(kv_give, 1, True)
    kv_far = other_core(kv_give)
    dq_part, near = cross_terms(True, core, before_near, q, lo)
    back_near = next_chip(near, -1, False)
    dq_part, far = cross_terms(False, core, before_far, q, lo, dq_part)
    back_far = next_chip(far, -1, True)
    own_far, near_dq, own_near = own_call(
        own_far_kernel, "own_far", [(4, bf16), (2, f32), (2, f32)], LOOKBACK_SPAN,
        core, kv_near, kv_far, q, lo, dq_part,
    )
    swapped = other_core(own_far)
    near_dq, own_near = own_call(
        own_near_kernel, "own_near", [(2, bf16), (2, f32)], HALF, core, kv_near, q, lo, near_dq, own_near
    )
    keys_shape = jax.ShapeDtypeStruct((HALF, 2 * HEAD_SIZE), bf16)
    queries_shape = jax.ShapeDtypeStruct((HALF, 4 * HEAD_SIZE), bf16)
    halves = join(join_near_kernel, "join_near", [keys_shape] * 2, 10000, core, own_near, back_near)
    return tuple(
        join(
            join_far_kernel, "join_far", [queries_shape, keys_shape, keys_shape], 1,
            core, near_dq, swapped, back_far, *halves,
        )
    )


def solution(mesh):
    seq, head = mesh.devices.shape
    fine = Mesh(mesh.devices.reshape(seq // CORES, CORES, head), ("chip", "core", "head"))
    tokens = ("chip", "core", "head")
    return jax.shard_map(
        on_device,
        mesh=fine,
        in_specs=(P(tokens), P(tokens), P(tokens), P(tokens), P(tokens), P(None, tokens), P()),
        out_specs=(P(("chip", "core"), "head"),) * 3,
        check_vma=False,
    )
```

```python
import functools
import math

import jax
import jax.numpy as jnp
from jax import lax
from jax.experimental import pallas as pl
from jax.experimental.pallas import tpu as pltpu
from jax.sharding import Mesh
from jax.sharding import PartitionSpec as P

HEAD_SIZE = 128
LOOKBACK_SPAN = 1024
CORES = 2
PIECE = 64
META_ROWS = 8
CHUNK = 128

score_scale = 168.0 ** (-0.5)
log2_e = math.log2(math.e)

f32 = jnp.float32
bf16 = jnp.bfloat16


def dot_t(left, right):
    return lax.dot_general(left, right, (((1,), (1,)), ((), ())), preferred_element_type=f32)


def dot_n(left, right):
    return lax.dot_general(left, right, (((1,), (0,)), ((), ())), preferred_element_type=f32)


def t_dot(left, right):
    return lax.dot_general(left, right, (((0,), (0,)), ((), ())), preferred_element_type=f32)


def pack_keys_kernel(key_ref, value_ref, out_ref):
    for at in range(CORES * out_ref.shape[1]):
        columns = slice(at * HEAD_SIZE, (at + 1) * HEAD_SIZE)
        out_ref[at % CORES, at // CORES, 0:PIECE, :] = key_ref[:, columns]
        out_ref[at % CORES, at // CORES, PIECE : 2 * PIECE, :] = value_ref[:, columns]


def pack_keys(keys, values, groups, steps=2):
    width = keys.shape[1] // steps
    return pl.pallas_call(
        pack_keys_kernel,
        grid=(steps,),
        in_specs=[pl.BlockSpec((PIECE, width), lambda i: (0, i))] * 2,
        out_specs=pl.BlockSpec((CORES, groups // steps, 2 * PIECE, HEAD_SIZE), lambda i: (0, i, 0, 0)),
        out_shape=jax.ShapeDtypeStruct((CORES, groups, 2 * PIECE, HEAD_SIZE), bf16),
        name="pack_keys",
    )(keys, values)


def three_parts(value):
    high = value.astype(bf16)
    rest = value - high.astype(f32)
    middle = rest.astype(bf16)
    return [high, middle, (rest - middle.astype(f32)).astype(bf16)]


def pack_queries_kernel(query_ref, grad_ref, row_ref, lse_ref, out_ref):
    groups = out_ref.shape[1]
    receivers = CORES * groups
    heads = 2 * receivers
    width = heads * HEAD_SIZE
    for at in range(receivers):
        for a in range(2):
            columns = slice((2 * at + a) * HEAD_SIZE, (2 * at + a + 1) * HEAD_SIZE)
            core, group = at % CORES, at // CORES
            out_ref[core, group, a * PIECE : (a + 1) * PIECE, :] = query_ref[:, columns]
            out_ref[core, group, (2 + a) * PIECE : (3 + a) * PIECE, :] = grad_ref[:, columns]
    product = grad_ref[...].astype(f32) * row_ref[...].astype(f32)
    product_high = product.astype(bf16)
    product_low = (product - product_high.astype(f32)).astype(bf16)
    which = lax.broadcasted_iota(jnp.int32, (heads, width), 1) // HEAD_SIZE
    member = jnp.where(which == lax.broadcasted_iota(jnp.int32, (heads, width), 0), 1.0, 0.0).astype(bf16)
    delta = dot_t(member, product_high) + dot_t(member, product_low)
    parts = three_parts(lse_ref[...]) + three_parts(delta)
    rows = jnp.concatenate([p.astype(f32) for p in parts], axis=0).astype(bf16)
    total = receivers * META_ROWS
    row_at = lax.broadcasted_iota(jnp.int32, (total, 6 * heads), 0)
    column_at = lax.broadcasted_iota(jnp.int32, (total, 6 * heads), 1)
    receiver = (row_at // META_ROWS) % groups * CORES + row_at // (META_ROWS * groups)
    halves = []
    for half in range(2):
        m = 2 * (row_at % META_ROWS) + half
        source = ((m // 6) * 3 + m % 3) * heads + 2 * receiver + (m // 3) % 2
        pick = jnp.where((m < 12) & (column_at == source), 1.0, 0.0).astype(bf16)
        halves.append(dot_n(pick, rows))
    meta = jnp.concatenate(halves, axis=1).reshape(CORES, groups, META_ROWS, HEAD_SIZE)
    for core in range(CORES):
        for group in range(groups):
            out_ref[core, group, 4 * PIECE : 4 * PIECE + META_ROWS, :] = meta[core, group].astype(bf16)


def pack_queries(queries, grads, rows, lse, groups, steps=4):
    width = queries.shape[1] // steps
    height = 4 * PIECE + META_ROWS
    return pl.pallas_call(
        pack_queries_kernel,
        grid=(steps,),
        in_specs=[pl.BlockSpec((PIECE, width), lambda i: (0, i))] * 3
        + [pl.BlockSpec((lse.shape[0] // steps, PIECE), lambda i: (i, 0))],
        out_specs=pl.BlockSpec((CORES, groups // steps, height, HEAD_SIZE), lambda i: (0, i, 0, 0)),
        out_shape=jax.ShapeDtypeStruct((CORES, groups, height, HEAD_SIZE), bf16),
        name="pack_queries",
    )(queries, grads, rows, lse)


def chunk_meta(ref, at):
    meta = [ref[2 * at + i, 4 * PIECE : 4 * PIECE + META_ROWS, :].astype(f32) for i in range(2)]
    turned = [pltpu.roll(m, PIECE, 1) for m in meta]
    left = lax.broadcasted_iota(jnp.int32, meta[0].shape, 1) < PIECE
    halves = (jnp.where(left, meta[0], turned[1]), jnp.where(left, turned[0], meta[1]))
    pieces = [halves[m % 2][m // 2 : m // 2 + 1] for m in range(12)]
    rows = [pieces[3 * r] + pieces[3 * r + 1] + pieces[3 * r + 2] for r in range(4)]
    return jnp.concatenate(rows[0:2], axis=1), jnp.concatenate(rows[2:4], axis=1)


def sweep(strips, causal, key_base, kv_ref, q_ref, lo_ref, dk_ref, dv_ref, dq_ref, part_ref, first_query=0):
    pieces = CHUNK // PIECE
    base = strips[0][1]
    for n, (at, first, last) in enumerate(strips):
        strip = slice((first - base) * CHUNK, (last - base) * CHUNK)
        height = (last - first) * CHUNK
        sources = slice(first * pieces, last * pieces)
        key = kv_ref[sources, 0:PIECE, :].reshape(height, HEAD_SIZE)
        value = kv_ref[sources, PIECE : 2 * PIECE, :].reshape(height, HEAD_SIZE)
        sources = slice(at * pieces, (at + 1) * pieces)

        def both(row):
            return jnp.concatenate(
                [q_ref[sources, (row + a) * PIECE : (row + a + 1) * PIECE, :].reshape(CHUNK, HEAD_SIZE) for a in range(2)]
            )

        query = both(0)
        grad = both(2)
        lse, delta = chunk_meta(q_ref, at)
        lse = lse * log2_e
        lo = lo_ref[at] - (key_base + first * CHUNK)
        lo = jnp.concatenate([lo, lo], axis=1)
        key_at = lax.broadcasted_iota(jnp.int32, (height, 2 * CHUNK), 0)
        allowed = key_at >= lo
        if causal:
            query_at = lax.broadcasted_iota(jnp.int32, (1, 2 * CHUNK), 1) % CHUNK + (at - first) * CHUNK
            allowed = allowed & (key_at <= query_at)
        scores = dot_t(key, query)
        prob = jnp.where(allowed, jnp.exp2(scores * (score_scale * log2_e) - lse), 0.0)
        prob_grad = dot_t(value, grad)
        score_grad = ((prob * score_scale) * (prob_grad - delta)).astype(bf16)
        dv = dot_n(prob.astype(bf16), grad)
        dk = dot_n(score_grad, query)
        if n == 0:
            dv_ref[strip, :] = dv
            dk_ref[strip, :] = dk
        else:
            dv_ref[strip, :] += dv
            dk_ref[strip, :] += dk
        dq = t_dot(score_grad, key)
        for a in range(2):
            mine = dq[a * CHUNK : (a + 1) * CHUNK]
            rows = slice((at - first_query) * CHUNK, (at - first_query + 1) * CHUNK)
            if part_ref is not None:
                mine = mine + part_ref[a, rows, :]
            dq_ref[a, rows, :] = mine


def cross_kernel(near, core_ref, kv_ref, q_ref, lo_ref, *refs):
    part_ref = None if near else refs[0]
    dq_ref, out_ref, dk_ref, dv_ref = refs[-4:]
    chunks = LOOKBACK_SPAN // CHUNK
    for block in range(CORES):

        @pl.when(core_ref[0] == (block if near else 1 - block))
        def _():
            start, end = block * chunks // CORES, (block + 1) * chunks // CORES
            sweep(
                [(at, max(at, start), end) for at in range(end)],
                False, 0, kv_ref, q_ref, lo_ref, dk_ref, dv_ref, dq_ref, part_ref,
            )
            rest = slice(end * CHUNK, LOOKBACK_SPAN)
            if end < chunks:
                dq_ref[:, rest, :] = jnp.zeros_like(dq_ref[:, rest, :]) if near else part_ref[:, rest, :]
            out_ref[0] = dk_ref[...].astype(bf16)
            out_ref[1] = dv_ref[...].astype(bf16)


def own_far_kernel(core_ref, kv_ref, q_ref, lo_ref, part_ref, far_ref, near_dq_ref, near_ref, dk_ref, dv_ref, dq_ref):
    chunks = LOOKBACK_SPAN // CHUNK
    half = chunks // CORES
    upper = [(at, 0, at + 1) for at in range(chunks - 1, half - 1, -1)]
    across = [(at, 0, half) for at in range(half, chunks)]
    lower = [(at, 0, at + 1) for at in range(half)]
    for core, strips in enumerate((upper, across + lower)):

        @pl.when(core_ref[0] == core)
        def _():
            sweep(
                strips, True, LOOKBACK_SPAN, kv_ref, q_ref, lo_ref, dk_ref, dv_ref, dq_ref, part_ref,
            )
            near = slice(core * HALF, (core + 1) * HALF)
            far = slice((1 - core) * HALF, (2 - core) * HALF)
            near_dq_ref[...] = part_ref[:, near, :] if core == 0 else dq_ref[:, near, :]
            far_ref[0:2] = dq_ref[:, far, :].astype(bf16)
            for i, sum_ref in enumerate((dk_ref, dv_ref)):
                far_ref[2 + i] = sum_ref[far, :].astype(bf16)
                near_ref[i] = sum_ref[near, :] if core == 0 else jnp.zeros_like(near_ref[i])


def own_near_kernel(core_ref, kv_ref, q_ref, lo_ref, part_dq_ref, part_ref, dq_out_ref, near_ref, dk_ref, dv_ref, dq_ref):
    chunks = LOOKBACK_SPAN // CHUNK
    half = chunks // CORES
    for core in range(CORES):

        @pl.when(core_ref[0] == core)
        def _():
            start = core * half
            sweep(
                [(at, start, at + 1) for at in range(start + half - 1, start - 1, -1)],
                True, LOOKBACK_SPAN, kv_ref, q_ref, lo_ref, dk_ref, dv_ref, dq_ref, part_dq_ref, start,
            )

    dq_out_ref[...] = dq_ref[...].astype(bf16)
    near_ref[0] = part_ref[0] + dk_ref[...]
    near_ref[1] = part_ref[1] + dv_ref[...]


def vmem_spec():
    return pl.BlockSpec(memory_space=pltpu.VMEM)


def smem_spec():
    return pl.BlockSpec(memory_space=pltpu.SMEM)


HALF = LOOKBACK_SPAN // CORES


def rows_scratch(rows):
    return [pltpu.VMEM((rows, HEAD_SIZE), f32)] * 2


def cost():
    pairs = LOOKBACK_SPAN * LOOKBACK_SPAN
    return pl.CostEstimate(flops=pairs * 5 * 2 * HEAD_SIZE, transcendentals=pairs, bytes_accessed=4 << 20)


def cross_terms(near, core, kv, q, lo, *part):
    return pl.pallas_call(
        functools.partial(cross_kernel, near),
        in_specs=[smem_spec()] + [vmem_spec()] * (3 + len(part)),
        out_specs=[vmem_spec()] * 2,
        out_shape=[
            jax.ShapeDtypeStruct((2, LOOKBACK_SPAN, HEAD_SIZE), f32),
            jax.ShapeDtypeStruct((2, HALF, HEAD_SIZE), bf16),
        ],
        scratch_shapes=rows_scratch(HALF),
        compiler_params=pltpu.CompilerParams(vmem_limit_bytes=20 << 20),
        cost_estimate=cost(),
        name="cross_near" if near else "cross_far",
    )(core, kv, q, lo, *part)


def own_call(kernel, name, shapes, rows, *operands):
    return pl.pallas_call(
        kernel,
        in_specs=[smem_spec()] + [vmem_spec()] * (len(operands) - 1),
        out_specs=[vmem_spec()] * len(shapes),
        out_shape=[jax.ShapeDtypeStruct((count, HALF, HEAD_SIZE), kind) for count, kind in shapes],
        scratch_shapes=rows_scratch(rows) + [pltpu.VMEM((2, rows, HEAD_SIZE), f32)],
        compiler_params=pltpu.CompilerParams(vmem_limit_bytes=20 << 20),
        cost_estimate=cost(),
        name=name,
    )(*operands)


def join_near_kernel(core_ref, near_ref, back_ref, dk_ref, dv_ref):
    for core in range(CORES):

        @pl.when(core_ref[0] == core)
        def _():
            columns = slice(core * HEAD_SIZE, (core + 1) * HEAD_SIZE)
            for i, out_ref in enumerate((dk_ref, dv_ref)):
                out_ref[:, columns] = (near_ref[i] + back_ref[i].astype(f32)).astype(bf16)


def join_queries_kernel(core_ref, near_ref, swapped_ref, dq_ref):
    for core in range(CORES):

        @pl.when(core_ref[0] == core)
        def _():
            for half_ref, k in ((near_ref, core), (swapped_ref, 1 - core)):
                for a in range(2):
                    at = 2 * k + a
                    dq_ref[:, at * HEAD_SIZE : (at + 1) * HEAD_SIZE] = half_ref[a]


def join_far_kernel(core_ref, swapped_ref, back_ref, near_dk_ref, near_dv_ref, dk_ref, dv_ref):
    for core in range(CORES):

        @pl.when(core_ref[0] == core)
        def _():
            near = slice(core * HEAD_SIZE, (core + 1) * HEAD_SIZE)
            far = slice((1 - core) * HEAD_SIZE, (2 - core) * HEAD_SIZE)
            for i, (half_ref, out_ref) in enumerate(((near_dk_ref, dk_ref), (near_dv_ref, dv_ref))):
                out_ref[:, near] = half_ref[:, near]
                out_ref[:, far] = (swapped_ref[2 + i].astype(f32) + back_ref[i].astype(f32)).astype(bf16)


def join(kernel, name, shapes, steps, *operands):
    return pl.pallas_call(
        kernel,
        in_specs=[smem_spec()] + [vmem_spec()] * (len(operands) - 1),
        out_specs=[vmem_spec()] * len(shapes),
        out_shape=shapes,
        compiler_params=pltpu.CompilerParams(vmem_limit_bytes=16 << 20),
        cost_estimate=pl.CostEstimate(flops=steps << 20, transcendentals=0, bytes_accessed=1 << 20),
        name=name,
    )(*operands)


def first_allowed(doc_ids, chip):
    padded = jnp.concatenate([jnp.full((LOOKBACK_SPAN,), -1, jnp.int32), doc_ids])
    window = lax.dynamic_slice_in_dim(padded, chip * LOOKBACK_SPAN, 2 * LOOKBACK_SPAN, 0)
    own = window[LOOKBACK_SPAN:]
    document_start = jnp.sum((window[:, None] < own[None, :]).astype(jnp.int32), axis=0)
    reach_start = jnp.arange(1, LOOKBACK_SPAN + 1, dtype=jnp.int32)
    return jnp.maximum(document_start, reach_start).reshape(LOOKBACK_SPAN // CHUNK, 1, CHUNK)


def exchange(value):
    value = value.reshape((-1,) + value.shape[2:])
    return lax.all_to_all(value, ("core", "head"), split_axis=0, concat_axis=0, tiled=True)


def on_device(queries, keys, values, rows, grads, lse, doc_ids):
    chips = lax.axis_size("chip")
    groups = lax.axis_size("head")
    chip = lax.axis_index("chip")
    core = lax.axis_index("core").astype(jnp.int32).reshape(1)
    lo = first_allowed(doc_ids, chip)
    kv = exchange(pack_keys(keys, values, groups))
    packed = pack_queries(queries, grads, rows, lse, groups)
    kv, packed = lax.optimization_barrier((kv, packed))
    q = exchange(packed)
    kv_before = lax.ppermute(kv, "chip", [(c, c + 1) for c in range(chips - 1)])
    dq_part, near = cross_terms(True, core, kv_before, q, lo)
    back_near = lax.ppermute(near, "chip", [(c + 1, c) for c in range(chips - 1)])
    dq_part, far = cross_terms(False, core, kv_before, q, lo, dq_part)
    back_far = lax.ppermute(
        far,
        ("chip", "core"),
        [(CORES * (c + 1) + k, CORES * c + 1 - k) for c in range(chips - 1) for k in range(CORES)],
    )
    own_far, near_dq, own_near = own_call(
        own_far_kernel, "own_far", [(4, bf16), (2, f32), (2, f32)], LOOKBACK_SPAN, core, kv, q, lo, dq_part
    )
    swapped = lax.ppermute(own_far, "core", [(0, 1), (1, 0)])
    near_dq, own_near = own_call(
        own_near_kernel, "own_near", [(2, bf16), (2, f32)], HALF, core, kv, q, lo, near_dq, own_near
    )
    keys_shape = jax.ShapeDtypeStruct((HALF, 2 * HEAD_SIZE), bf16)
    queries_shape = jax.ShapeDtypeStruct((HALF, 4 * HEAD_SIZE), bf16)
    halves = join(join_near_kernel, "join_near", [keys_shape] * 2, 10000, core, own_near, back_near)
    (query_grad,) = join(join_queries_kernel, "join_queries", [queries_shape], 1000, core, near_dq, swapped)
    key_grad, value_grad = join(join_far_kernel, "join_far", [keys_shape] * 2, 1, core, swapped, back_far, *halves)
    return query_grad, key_grad, value_grad


def solution(mesh):
    seq, head = mesh.devices.shape
    fine = Mesh(mesh.devices.reshape(seq // CORES, CORES, head), ("chip", "core", "head"))
    tokens = ("chip", "core", "head")
    return jax.shard_map(
        on_device,
        mesh=fine,
        in_specs=(P(tokens), P(tokens), P(tokens), P(tokens), P(tokens), P(None, tokens), P()),
        out_specs=(P(("chip", "core"), "head"),) * 3,
        check_vma=False,
    )
```
